128 devices in a mesh: tm: 8 (over x, core), space: 16 (over y, z).
Axes of the slice: x: 4, y: 4, z: 4, core: 2. Of those that a mesh axis runs over, the one named last changes fastest.
Arguments:
- source: float32 [8, 128, 256, 128], P('tm', 'space'), may hold values from -24 to 24
- initial: float32 [128, 256, 128], P('space'), may hold values from -24 to 24
- diffusivity: float32 [128, 256, 128], P('space'), may hold values from 0.5 to 6, as said below
Outputs:
- field_steps: float32 [8, 128, 256, 128], P('tm', 'space')
The draws below stay inside these ranges and needn't reach their ends.
Inputs may be any that keep to these rules, and one draw needn't show every extreme that they name: The diffusivity at every cell, positive.
All inputs are finite; a program needn't handle non-finite values.
Results may differ from the reference program's by a relative error of at most 0.0003.
Values sent between devices are 32-bit elements; how exact they have to be, the bound alone decides.
No kernel may reach another device: no remote copies, remote signals or barrier semaphores. Data moves between devices by JAX's collectives and lax.ppermute only.
A program may use at most 128 MiB of HBM per device.

```python
import math
import jax
import jax.numpy as jnp

NX = 128
NY = 256
NZ = 128
STEPS = 8


def draw_diffusivity(key, part):
    base = jnp.exp(jax.random.uniform(key, (NX, NY, NZ), jnp.float32, math.log(0.5), math.log(2.0)))
    ramp = 1.0 + 2.0 * jnp.arange(NX, dtype=jnp.float32) / (NX - 1)
    return base * ramp[:, None, None]


def steps_of(stream_key, extent, cuts, smallest, largest):
    level, own = 1.0, jax.random.fold_in(stream_key, 6)
    for position, parts in cuts:
        draws = jnp.exp(jax.random.uniform(jax.random.fold_in(own, position), (parts,), jnp.float32, smallest / len(cuts), largest / len(cuts)))
        level = level * jnp.repeat(draws, extent[position] // parts).reshape([-1 if axis == position else 1 for axis in range(len(extent))])
    return level


def bell_draw(key, shape, width, bound, cuts=(), kind=jnp.bfloat16):
    values = width * jax.random.normal(key, shape, jnp.float32)
    if cuts:
        values = values * steps_of(key, shape, cuts, -0.22, 0.18)
    return jnp.clip(values, -bound, bound).astype(kind)


def setup_inputs(seed: int = 0) -> dict:
    arg_keys = jax.random.split(jax.random.key(seed), 4)
    return {
        "source": bell_draw(arg_keys[0], (STEPS, NX, NY, NZ), 4.0, 24.0, ((0, 8), (1, 16)), jnp.float32),
        "initial": bell_draw(arg_keys[1], (NX, NY, NZ), 4.0, 24.0, ((0, 16),), jnp.float32),
        "diffusivity": draw_diffusivity(jax.random.fold_in(arg_keys[3], 71), 0),
    }


alpha_corner = 0.05
step_length = 1.0

def face_terms(diffusivity):
    listed = []
    for dimension in range(3):
        listed.append(0.5 * (diffusivity + jnp.roll(diffusivity, -1, dimension)))
        listed.append(0.5 * (diffusivity + jnp.roll(diffusivity, 1, dimension)))
    return listed

def diffuse(values, terms):
    accumulated = terms[0] * (values - jnp.roll(values, -1, 0)) + terms[1] * (values - jnp.roll(values, 1, 0))
    accumulated = accumulated + terms[2] * (values - jnp.roll(values, -1, 1)) + terms[3] * (values - jnp.roll(values, 1, 1))
    accumulated = accumulated + terms[4] * (values - jnp.roll(values, -1, 2)) + terms[5] * (values - jnp.roll(values, 1, 2))
    return accumulated

def apply_system(vec_real, vec_imag, terms, shift):
    out_real = shift[0] * vec_real - shift[1] * vec_imag + step_length * diffuse(vec_real, terms)
    out_imag = shift[0] * vec_imag + shift[1] * vec_real + step_length * diffuse(vec_imag, terms)
    return (out_real, out_imag)

def wave_symbol(count, dtype):
    return 4.0 * jnp.sin(math.pi * jnp.arange(count, dtype=dtype) / count) ** 2

def precondition(vec_real, vec_imag, shift, mean_kappa):
    full_x, full_y, full_z = vec_real.shape
    spectrum = jnp.fft.fftn(vec_real + 1j * vec_imag)
    symbol = wave_symbol(full_x, vec_real.dtype)[:, None, None] + wave_symbol(full_y, vec_real.dtype)[None, :, None]
    symbol = symbol + wave_symbol(full_z, vec_real.dtype)[None, None, :]
    denom_real = shift[0] + step_length * mean_kappa * symbol
    denom_imag = shift[1]
    magnitude = denom_real * denom_real + denom_imag * denom_imag
    spec_real = jnp.real(spectrum).astype(vec_real.dtype)
    spec_imag = jnp.imag(spectrum).astype(vec_real.dtype)
    ratio_real = (spec_real * denom_real + spec_imag * denom_imag) / magnitude
    ratio_imag = (spec_imag * denom_real - spec_real * denom_imag) / magnitude
    result = jnp.fft.ifftn(ratio_real + 1j * ratio_imag)
    return (jnp.real(result).astype(vec_real.dtype), jnp.imag(result).astype(vec_real.dtype))

def inner_product(left_real, left_imag, right_real, right_imag):
    return (jnp.sum(left_real * right_real + left_imag * right_imag), jnp.sum(left_real * right_imag - left_imag * right_real))

def remove_part(vec_real, vec_imag, factor, basis_real, basis_imag):
    return (vec_real - (factor[0] * basis_real - factor[1] * basis_imag), vec_imag - (factor[0] * basis_imag + factor[1] * basis_real))

def small_solve(rhs_norm, first_diag, first_sub, second_top, second_diag, second_sub):
    gram_first = first_diag[0] * first_diag[0] + first_diag[1] * first_diag[1] + first_sub * first_sub
    gram_second = second_top[0] * second_top[0] + second_top[1] * second_top[1] + second_diag[0] * second_diag[0] + second_diag[1] * second_diag[1] + second_sub * second_sub
    cross_real = first_diag[0] * second_top[0] + first_diag[1] * second_top[1] + first_sub * second_diag[0]
    cross_imag = first_diag[0] * second_top[1] - first_diag[1] * second_top[0] + first_sub * second_diag[1]
    target_one = (rhs_norm * first_diag[0], -rhs_norm * first_diag[1])
    target_two = (rhs_norm * second_top[0], -rhs_norm * second_top[1])
    determinant = gram_first * gram_second - (cross_real * cross_real + cross_imag * cross_imag)
    coef_one = ((gram_second * target_one[0] - (cross_real * target_two[0] - cross_imag * target_two[1])) / determinant, (gram_second * target_one[1] - (cross_real * target_two[1] + cross_imag * target_two[0])) / determinant)
    coef_two = ((gram_first * target_two[0] - (cross_real * target_one[0] + cross_imag * target_one[1])) / determinant, (gram_first * target_two[1] - (cross_real * target_one[1] - cross_imag * target_one[0])) / determinant)
    return (coef_one, coef_two)

def krylov_solve(rhs_real, rhs_imag, terms, shift, mean_kappa):
    rhs_norm = jnp.sqrt(jnp.sum(rhs_real * rhs_real + rhs_imag * rhs_imag))
    first_real, first_imag = (rhs_real / rhs_norm, rhs_imag / rhs_norm)
    pre_one = precondition(first_real, first_imag, shift, mean_kappa)
    work_real, work_imag = apply_system(pre_one[0], pre_one[1], terms, shift)
    first_diag = inner_product(first_real, first_imag, work_real, work_imag)
    work_real, work_imag = remove_part(work_real, work_imag, first_diag, first_real, first_imag)
    first_sub = jnp.sqrt(jnp.sum(work_real * work_real + work_imag * work_imag))
    second_real, second_imag = (work_real / first_sub, work_imag / first_sub)
    pre_two = precondition(second_real, second_imag, shift, mean_kappa)
    work_real, work_imag = apply_system(pre_two[0], pre_two[1], terms, shift)
    second_top = inner_product(first_real, first_imag, work_real, work_imag)
    work_real, work_imag = remove_part(work_real, work_imag, second_top, first_real, first_imag)
    second_diag = inner_product(second_real, second_imag, work_real, work_imag)
    work_real, work_imag = remove_part(work_real, work_imag, second_diag, second_real, second_imag)
    second_sub = jnp.sqrt(jnp.sum(work_real * work_real + work_imag * work_imag))
    coef_one, coef_two = small_solve(rhs_norm, first_diag, first_sub, second_top, second_diag, second_sub)
    sol_real = coef_one[0] * pre_one[0] - coef_one[1] * pre_one[1] + coef_two[0] * pre_two[0] - coef_two[1] * pre_two[1]
    sol_imag = coef_one[0] * pre_one[1] + coef_one[1] * pre_one[0] + coef_two[0] * pre_two[1] + coef_two[1] * pre_two[0]
    return (sol_real, sol_imag)

def reference(source, initial, diffusivity):
    steps = source.shape[0]
    terms = face_terms(diffusivity)
    mean_kappa = jnp.mean(diffusivity)
    lifted = step_length * source
    lifted = lifted.at[0].add(initial)
    ramp = jnp.arange(steps, dtype=source.dtype) / steps
    lifted = lifted * (alpha_corner ** ramp)[:, None, None, None]
    spectrum = jnp.fft.fft(lifted, axis=0)
    decay_root = alpha_corner ** (1.0 / steps)
    solved = []
    for frequency in range(steps):
        phase_angle = 2.0 * math.pi * frequency / steps
        shift = (1.0 - decay_root * math.cos(phase_angle), decay_root * math.sin(phase_angle))
        rhs_real = jnp.real(spectrum[frequency]).astype(source.dtype)
        rhs_imag = jnp.imag(spectrum[frequency]).astype(source.dtype)
        sol_real, sol_imag = krylov_solve(rhs_real, rhs_imag, terms, shift, mean_kappa)
        solved.append(sol_real + 1j * sol_imag)
    restored = jnp.fft.ifft(jnp.stack(solved), axis=0)
    return jnp.real(restored).astype(source.dtype) * (alpha_corner ** (-ramp))[:, None, None, None]
```

```python
import functools
import math

import jax
import jax.numpy as jnp
import numpy as np
from jax import lax
from jax.experimental import pallas as pl
from jax.experimental.pallas import tpu as pltpu
from jax.sharding import PartitionSpec as P


alpha_corner = 0.05
step_length = 1.0
BOTH = ("tm", "space")
NX, NY, NZ = 128, 256, 128
STEPS = 8
SLABS = 16
DEVS = 128
f32 = jnp.float32
bf16 = jnp.bfloat16
ROOT = alpha_corner ** (1.0 / STEPS)
HALF = math.sqrt(0.5)


def cas_table(length):
    index = np.arange(length)
    phase = (index[:, None] * index[None, :] % length) * (2.0 * np.pi / length)
    return (np.cos(phase) + np.sin(phase)) / math.sqrt(length)


def halves(table):
    table = np.asarray(table, np.float32)
    high = table.astype(bf16)
    low = (table - high.astype(np.float32)).astype(bf16)
    return np.stack([high, low])


def symbol_row(length):
    return 4.0 * np.sin(np.pi * np.arange(length) / length) ** 2


def tables():
    cas_x, cas_y, cas_z = cas_table(NX), cas_table(NY), cas_table(NZ)
    row = np.arange(NX)
    gathered = 8 * (row % 16) + row // 16
    row = np.arange(6 * 32)
    spread = (8 * (row % 16) + 4 * (row // 16 % 2) + row // 32 - 1) % NX
    return {
        "x_in": halves(cas_x[:, gathered]),
        "x_spread": halves(cas_x[spread, :]),
        "x": halves(cas_x),
        "y": halves(cas_y),
        "z": halves(cas_z),
        "symbol": np.asarray(symbol_row(NX)[:, None] + symbol_row(NY)[None, :], np.float32),
    }


def shift_of(frequency):
    phase = 2.0 * math.pi * frequency / STEPS
    return (1.0 - ROOT * math.cos(phase), ROOT * math.sin(phase) if frequency % 4 else 0.0)


def split(value):
    high = value.astype(bf16)
    return high, (value - high.astype(f32)).astype(bf16)


def dot(left, right):
    return jnp.dot(left, right, preferred_element_type=f32)


def left_mul(table_ref, value):
    high, low = split(value)
    return dot(table_ref[0], high) + (dot(table_ref[0], low) + dot(table_ref[1], high))


def right_mul(value, table_ref):
    high, low = split(value)
    return dot(high, table_ref[0]) + (dot(low, table_ref[0]) + dot(high, table_ref[1]))


def vmem():
    return pl.BlockSpec(memory_space=pltpu.VMEM)


def smem():
    return pl.BlockSpec(memory_space=pltpu.SMEM)


def shape(*dims):
    return jax.ShapeDtypeStruct(dims, f32)


def enter_kernel(first_ref, source_ref, initial_ref, kappa_ref, z_ref, out_ref):
    first = first_ref[0]
    total = jnp.zeros((8, 128), f32)
    nt = (((1,), (1,)), ((), ()))
    for x in range(8):
        value = source_ref[x] + first * initial_ref[x]
        high, low = split(value)
        dims = functools.partial(lax.dot_general, dimension_numbers=nt, preferred_element_type=f32)
        freq = dims(z_ref[0], high) + (dims(z_ref[0], low) + dims(z_ref[1], high))
        for yh in range(2):
            for block in range(16):
                out_ref[pl.ds(block * 8 * 17 + yh * 8 + x, 8, stride=17), :] = freq[
                    block * 8 : block * 8 + 8, yh * 128 : yh * 128 + 128
                ]
        total = total + jnp.sum(kappa_ref[x].reshape(32, 8, 128), axis=0)
    whole = jnp.broadcast_to(jnp.sum(total, keepdims=True), (8, 128))
    for block in range(16):
        out_ref[pl.ds(block * 8 * 17 + 16, 8, stride=17), :] = whole


def precondition_fields(work, kappa, symbol_z, symbol_ref, out):
    symbol = symbol_ref[...] + symbol_z
    scaled = step_length * kappa * symbol
    for pair in range(4):
        first = work[pl.ds(pair * 256, 128), :]
        second = work[pl.ds(pair * 256 + 128, 128), :]
        if pair == 0:
            out[pl.ds(0, 128), :] = first / (shift_of(0)[0] + scaled)
            out[pl.ds(128, 128), :] = second / (shift_of(4)[0] + scaled)
        else:
            shift = shift_of(pair)
            denom = shift[0] + scaled
            inverse = 1.0 / (denom * denom + shift[1] * shift[1])
            real, imag = denom * inverse, shift[1] * inverse
            out[pl.ds(pair * 256, 128), :] = first * real + second * imag
            out[pl.ds(pair * 256 + 128, 128), :] = second * real - first * imag


def spectral_core(kappa, symbol_z, gathered, x_in_ref, x_spread_ref, y_ref, symbol_ref, hat_ref, out_ref, work):
    for field in range(8):
        work[pl.ds(field * 128, 128), :] = left_mul(x_in_ref, gathered[pl.ds(field * 128, 128), :])
    work[...] = right_mul(work[...], y_ref)
    precondition_fields(work, kappa, symbol_z, symbol_ref, hat_ref)
    work[...] = right_mul(hat_ref[...], y_ref)
    for field in range(8):
        spread = left_mul(x_spread_ref, work[pl.ds(field * 128, 128), :])
        pair, part = field // 2, field % 2
        for x in range(6):
            for core in range(2):
                for block in range(2):
                    row = (x * 2 + core) * 16 + block * 8
                    base = ((2 * pair + core) * 16 + block * 8) * 24 + part * 6 + x
                    for yh in range(2):
                        out_ref[pl.ds(base + yh * 12, 8, stride=24), :] = spread[
                            row : row + 8, yh * 128 : yh * 128 + 128
                        ]


def spectral_first_kernel(
    symbol_z_ref, in_ref, x_in_ref, x_spread_ref, y_ref, symbol_ref, hat_ref, out_ref, kappa_ref, gathered, work
):
    parts = in_ref[pl.ds(16, 8, stride=17), :] + in_ref[pl.ds(16 + 8 * 17, 8, stride=17), :]
    kappa = jnp.sum(parts, axis=0, keepdims=True) * (1.0 / (NX * NY * NZ))
    kappa_ref[...] = jnp.broadcast_to(kappa, (8, 128))
    kappa = kappa[:, 0:1]
    for x in range(8):
        for block in range(2):
            for yh in range(2):
                lifted = []
                for step in range(8):
                    row = (step * 16 + block * 8) * 17 + yh * 8 + x
                    lifted.append(in_ref[pl.ds(row, 8, stride=17), :] * (alpha_corner ** (step / STEPS)))
                plus = [lifted[m] + lifted[m + 4] for m in range(4)]
                minus = [lifted[m] - lifted[m + 4] for m in range(4)]
                odd_minus = HALF * (minus[1] - minus[3])
                odd_plus = HALF * (minus[1] + minus[3])
                even, odd = plus[0] + plus[2], plus[1] + plus[3]
                fields = [
                    even + odd,
                    even - odd,
                    minus[0] + odd_minus,
                    -minus[2] - odd_plus,
                    plus[0] - plus[2],
                    plus[3] - plus[1],
                    minus[0] - odd_minus,
                    minus[2] - odd_plus,
                ]
                for field in range(8):
                    gathered[pl.ds(field * 128 + x * 16 + block * 8, 8), pl.ds(yh * 128, 128)] = fields[field]
    spectral_core(
        kappa, symbol_z_ref[0], gathered, x_in_ref, x_spread_ref, y_ref, symbol_ref, hat_ref, out_ref, work
    )


def spectral_second_kernel(
    symbol_z_ref, kappa_ref, in_ref, x_in_ref, x_spread_ref, y_ref, symbol_ref, hat_ref, out_ref, gathered, work
):
    for field in range(8):
        pair, part = field // 2, field % 2
        for core in range(2):
            for x in range(4):
                for block in range(2):
                    for yh in range(2):
                        row = ((2 * pair + core) * 16 + block * 8) * 16 + yh * 8 + part * 4 + x
                        gathered[
                            pl.ds(field * 128 + (core * 4 + x) * 16 + block * 8, 8), pl.ds(yh * 128, 128)
                        ] = in_ref[pl.ds(row, 8, stride=16), :]
    kappa = kappa_ref[0:1, 0:1]
    spectral_core(
        kappa, symbol_z_ref[0], gathered, x_in_ref, x_spread_ref, y_ref, symbol_ref, hat_ref, out_ref, work
    )


def coefficients(sums):
    lane = lax.broadcasted_iota(jnp.int32, (4, 128), 1)

    def pick(number):
        return jnp.sum(jnp.where(lane == number, sums, 0.0), axis=1, keepdims=True)

    values = [pick(number) for number in range(16)]
    packed = lax.broadcasted_iota(jnp.int32, (4, 1), 0) == 0

    def complex_of(base):
        return values[base] + values[base + 1], values[base + 2] - values[base + 3]

    def solve(g11, g22, g12, h1, h2):
        scale1 = jnp.where(g11 > 0.0, lax.rsqrt(jnp.maximum(g11, 1e-37)), 0.0)
        scale2 = jnp.where(g22 > 0.0, lax.rsqrt(jnp.maximum(g22, 1e-37)), 0.0)
        corr = (g12[0] * scale1 * scale2, g12[1] * scale1 * scale2)
        t1 = (h1[0] * scale1, h1[1] * scale1)
        t2 = (h2[0] * scale2, h2[1] * scale2)
        det = 1.0 - (corr[0] * corr[0] + corr[1] * corr[1])
        good = jnp.logical_and(det > 1e-6, g22 > 0.0)
        inv = jnp.where(good, 1.0 / jnp.where(good, det, 1.0), 0.0)
        one = (
            jnp.where(good, (t1[0] - (corr[0] * t2[0] - corr[1] * t2[1])) * inv, t1[0]),
            jnp.where(good, (t1[1] - (corr[0] * t2[1] + corr[1] * t2[0])) * inv, t1[1]),
        )
        two = (
            (t2[0] - (corr[0] * t1[0] + corr[1] * t1[1])) * inv,
            (t2[1] - (corr[0] * t1[1] - corr[1] * t1[0])) * inv,
        )
        return (1.0 - one[0] * scale1, -one[1] * scale1), (-two[0] * scale2, -two[1] * scale2)

    zero = jnp.zeros((4, 1), f32)
    full = solve(values[0] + values[1], values[2] + values[3], complex_of(4), complex_of(8), complex_of(12))
    first = solve(values[0], values[2], (values[4], zero), (values[8], zero), (values[12], zero))
    second = solve(values[1], values[3], (values[5], zero), (values[9], zero), (values[13], zero))
    maps = []
    for vector in range(2):
        maps.append(
            (
                jnp.where(packed, first[vector][0], full[vector][0]),
                jnp.where(packed, 0.0, full[vector][1]),
                jnp.where(packed, second[vector][0], full[vector][0]),
            )
        )
    return maps


def spectral_last_kernel(sums_ref, hat_one_ref, hat_two_ref, x_ref, y_ref, out_ref, work):
    sums = jnp.concatenate(
        [jnp.sum(sums_ref[pl.ds(pair * 32, 32), :], axis=0, keepdims=True) for pair in range(4)], axis=0
    )
    maps = coefficients(sums)
    scales = [[[entry[pair : pair + 1, :] for entry in vector] for pair in range(4)] for vector in maps]
    for block in range(16):
        rows = 8
        fields = []
        for pair in range(4):
            parts = []
            for hat in (hat_one_ref, hat_two_ref):
                parts.append(
                    (
                        hat[pl.ds(pair * 256 + block * rows, rows), :],
                        hat[pl.ds(pair * 256 + 128 + block * rows, rows), :],
                    )
                )
            (p1, q1), (p2, q2) = parts
            (a1, b1, c1), (a2, b2, c2) = scales[0][pair], scales[1][pair]
            fields.append(a1 * p1 - b1 * q1 + (a2 * p2 - b2 * q2))
            fields.append(c1 * q1 + b1 * p1 + (c2 * q2 + b2 * p2))
        zero, four, re1, im1, re2, im2, re3, im3 = fields
        even = [zero + four + 2.0 * re2, zero - four - 2.0 * im2, zero + four - 2.0 * re2, zero - four + 2.0 * im2]
        diff, total = (2.0 * HALF) * (re1 - re3), (2.0 * HALF) * (im1 + im3)
        odd = [2.0 * (re1 + re3), diff - total, 2.0 * (im3 - im1), -diff - total]
        for step in range(8):
            value = even[step % 4] + odd[step % 4] if step < 4 else even[step % 4] - odd[step % 4]
            scale = alpha_corner ** (-step / STEPS) / STEPS
            work[pl.ds(step * 128 + block * rows, rows), :] = value * scale
    work[...] = right_mul(work[...], y_ref)
    for step in range(8):
        planes = left_mul(x_ref, work[pl.ds(step * 128, 128), :])
        for slab in range(16):
            for yh in range(2):
                out_ref[pl.ds((step * 16 + slab) * 16 + yh * 8, 8), :] = planes[
                    slab * 8 : slab * 8 + 8, yh * 128 : yh * 128 + 128
                ]


def faces_kernel(core_ref, kappa_ref, rim_ref, x_face_ref, y_face_ref, z_face_ref, planes):
    core = core_ref[0]
    rim = rim_ref[0]
    for x in range(6):
        if x == 0:
            plane = jnp.where(core == 0, rim, kappa_ref[3])
        elif x == 5:
            plane = jnp.where(core == 0, kappa_ref[4], rim)
        else:
            plane = kappa_ref[4 * core + x - 1]
        planes[x] = plane.T
    for x in range(5):
        x_face_ref[x] = 0.5 * (planes[x] + planes[x + 1])
    for x in range(4):
        plane = planes[x + 1]
        y_face_ref[x] = 0.5 * (plane + pltpu.roll(plane, NY - 1, 1))
        z_face_ref[x] = 0.5 * (plane + pltpu.roll(plane, NZ - 1, 0))


def load_block(in_ref, z_ref, field):
    for part in range(2):
        for x in range(6):
            columns = []
            for yh in range(2):
                rows = [in_ref[pl.ds(block * 8 * 24 + yh * 12 + part * 6 + x, 8, stride=24), :] for block in range(16)]
                columns.append(jnp.concatenate(rows, axis=0))
            field[part, x] = left_mul(z_ref, jnp.concatenate(columns, axis=1))


def difference(field, part, x, kappa, x_face_ref, y_face_ref, z_face_ref):
    here = field[part, x + 1]
    flux_low = (x_face_ref[x] - kappa) * (here - field[part, x])
    flux_high = (x_face_ref[x + 1] - kappa) * (field[part, x + 2] - here)
    flux_y = (y_face_ref[x] - kappa) * (pltpu.roll(here, NY - 1, 1) - here)
    flux_z = (z_face_ref[x] - kappa) * (pltpu.roll(here, NZ - 1, 0) - here)
    return (
        (flux_low - flux_high) + (pltpu.roll(flux_y, 1, 1) - flux_y) + (pltpu.roll(flux_z, 1, 0) - flux_z)
    )


def constant_part(field, part, x):
    here = field[part, x + 1]
    around = field[part, x] + field[part, x + 2]
    around = around + pltpu.roll(here, NY - 1, 1) + pltpu.roll(here, 1, 1)
    around = around + pltpu.roll(here, NZ - 1, 0) + pltpu.roll(here, 1, 0)
    return 6.0 * here - around


def block_first_kernel(
    shift_ref, kappa_ref, in_ref, z_ref, x_face_ref, y_face_ref, z_face_ref, out_ref, differ_ref, right_ref, field
):
    kappa = kappa_ref[0:1, 0:1]
    load_block(in_ref, z_ref, field)
    for x in range(4):
        for part in range(2):
            value = difference(field, part, x, kappa, x_face_ref, y_face_ref, z_face_ref)
            differ_ref[part, x] = value
            freq = left_mul(z_ref, value)
            for yh in range(2):
                for block in range(16):
                    out_ref[pl.ds(block * 8 * 16 + yh * 8 + part * 4 + x, 8, stride=16), :] = freq[
                        block * 8 : block * 8 + 8, yh * 128 : yh * 128 + 128
                    ]
            here, other = field[part, x + 1], field[1 - part, x + 1]
            cross = -shift_ref[2] if part == 0 else shift_ref[2]
            right_ref[part, x] = (
                shift_ref[part] * here + cross * other + (step_length * kappa) * constant_part(field, part, x)
            )


def block_second_kernel(
    kappa_ref, in_ref, differ_ref, right_ref, z_ref, x_face_ref, y_face_ref, z_face_ref, out_ref, field
):
    kappa = kappa_ref[0:1, 0:1]
    load_block(in_ref, z_ref, field)
    totals = [jnp.zeros((8, 256), f32) for _ in range(16)]

    def fold(value):
        return jnp.sum(value.reshape(16, 8, 256), axis=0)

    for x in range(4):
        diffs = [differ_ref[part, x] for part in range(2)]
        ones = [right_ref[part, x] + diffs[part] for part in range(2)]
        twos = [
            diffs[part] + difference(field, part, x, kappa, x_face_ref, y_face_ref, z_face_ref) for part in range(2)
        ]
        pairs = [(ones[0], ones[0]), (ones[1], ones[1]), (twos[0], twos[0]), (twos[1], twos[1])]
        for left, right in ((ones, twos), (ones, diffs), (twos, diffs)):
            pairs += [(left[0], right[0]), (left[1], right[1]), (left[0], right[1]), (left[1], right[0])]
        for number, (left, right) in enumerate(pairs):
            totals[number] = totals[number] + fold(left * right)
    lane = lax.broadcasted_iota(jnp.int32, (1, 128), 1)
    row = jnp.zeros((1, 128), f32)
    for number in range(16):
        row = row + jnp.where(lane == number, jnp.sum(totals[number], keepdims=True), 0.0)
    out_ref[...] = jnp.broadcast_to(row, (DEVS, 128))


def leave_kernel(in_ref, z_ref, out_ref):
    tn = (((0,), (0,)), ((), ()))
    dims = functools.partial(lax.dot_general, dimension_numbers=tn, preferred_element_type=f32)
    for x in range(8):
        columns = []
        for yh in range(2):
            rows = [in_ref[pl.ds(block * 8 * 16 + yh * 8 + x, 8, stride=16), :] for block in range(16)]
            columns.append(jnp.concatenate(rows, axis=0))
        value = left_mul(z_ref, jnp.concatenate(columns, axis=1))
        out_ref[0, x] = value.T


def exchange(rows):
    wide = rows.reshape(rows.shape[0], 1, 128)
    return lax.all_to_all(wide, BOTH, split_axis=0, concat_axis=0, tiled=True).reshape(rows.shape)


def call(kernel, outs, scalars, scratch, *args):
    return pl.pallas_call(
        kernel,
        out_shape=outs,
        in_specs=[smem()] * scalars + [vmem()] * (len(args) - scalars),
        out_specs=jax.tree.map(lambda _: vmem(), outs),
        scratch_shapes=scratch,
        name=kernel.__name__,
    )(*args)


def shards(source, initial, diffusivity):
    table = tables()
    position = lax.axis_index("tm")
    slab = lax.axis_index("space")
    core = position % 2
    pair = position // 2
    first = jnp.where(position == 0, step_length / step_length, 0.0).astype(f32).reshape(1)
    wave = (position * SLABS + slab).astype(f32)
    symbol_z = (4.0 * jnp.sin(math.pi * wave / NZ) ** 2).reshape(1)
    real = jnp.asarray([shift_of(k)[0] for k in range(4)], f32)[pair]
    imag = jnp.asarray([shift_of(k)[1] for k in range(4)], f32)[pair]
    other = jnp.where(pair == 0, shift_of(4)[0], real)
    shift = jnp.stack([real, other, imag]).astype(f32)

    rim_out = jnp.where(core == 0, diffusivity[7], diffusivity[0])[None]
    route = []
    for time in range(STEPS):
        for node in range(SLABS):
            step = 1 if time % 2 == 0 else SLABS - 1
            route.append((time * SLABS + node, time * SLABS + (node + step) % SLABS))
    rim = lax.ppermute(rim_out, BOTH, route)
    faces = call(
        faces_kernel,
        [shape(5, NZ, NY), shape(4, NZ, NY), shape(4, NZ, NY)],
        1,
        [pltpu.VMEM((6, NZ, NY), f32)],
        core.astype(jnp.int32).reshape(1),
        diffusivity,
        rim,
    )

    rows = call(enter_kernel, shape(DEVS * 17, 128), 1, [], first, source[0], initial, diffusivity, table["z"])
    rows = exchange(rows)
    big = pltpu.VMEM((1024, NY), f32)
    hat_one, rows, kappa = call(
        spectral_first_kernel,
        [shape(1024, NY), shape(DEVS * 24, 128), shape(8, 128)],
        1,
        [big, big],
        symbol_z,
        rows,
        table["x_in"],
        table["x_spread"],
        table["y"],
        table["symbol"],
    )
    rows = exchange(rows)
    block = pltpu.VMEM((2, 6, NZ, NY), f32)
    rows, differ, right = call(
        block_first_kernel,
        [shape(DEVS * 16, 128), shape(2, 4, NZ, NY), shape(2, 4, NZ, NY)],
        1,
        [block],
        shift,
        kappa,
        rows,
        table["z"],
        *faces,
    )
    rows = exchange(rows)
    hat_two, rows = call(
        spectral_second_kernel,
        [shape(1024, NY), shape(DEVS * 24, 128)],
        1,
        [big, big],
        symbol_z,
        kappa,
        rows,
        table["x_in"],
        table["x_spread"],
        table["y"],
        table["symbol"],
    )
    rows = exchange(rows)
    sums = call(
        block_second_kernel, shape(DEVS, 128), 0, [block], kappa, rows, differ, right, table["z"], *faces
    )
    sums = exchange(sums)
    rows = call(
        spectral_last_kernel, shape(DEVS * 16, 128), 0, [big], sums, hat_one, hat_two, table["x"], table["y"]
    )
    rows = exchange(rows)
    return call(leave_kernel, shape(1, 8, NY, NZ), 0, [], rows, table["z"])


def solution(mesh):
    in_specs = (P("tm", "space", None, None), P("space", None, None), P("space", None, None))
    out_specs = P("tm", "space", None, None)
    return jax.shard_map(shards, mesh=mesh, in_specs=in_specs, out_specs=out_specs, check_vma=False)
```

```python
import functools
import math

import jax
import jax.numpy as jnp
import numpy as np
from jax import lax
from jax.experimental import pallas as pl
from jax.experimental.pallas import tpu as pltpu
from jax.sharding import PartitionSpec as P


alpha_corner = 0.05
step_length = 1.0
BOTH = ("tm", "space")
NX, NY, NZ = 128, 256, 128
STEPS = 8
SLABS = 16
DEVS = 128
f32 = jnp.float32
bf16 = jnp.bfloat16
ROOT = alpha_corner ** (1.0 / STEPS)
HALF = math.sqrt(0.5)


def cas_table(length):
    index = np.arange(length)
    phase = (index[:, None] * index[None, :] % length) * (2.0 * np.pi / length)
    return (np.cos(phase) + np.sin(phase)) / math.sqrt(length)


def halves(table):
    table = np.asarray(table, np.float32)
    high = table.astype(bf16)
    low = (table - high.astype(np.float32)).astype(bf16)
    return np.stack([high, low])


def symbol_row(length):
    return 4.0 * np.sin(np.pi * np.arange(length) / length) ** 2


def tables():
    cas_x, cas_y, cas_z = cas_table(NX), cas_table(NY), cas_table(NZ)
    row = np.arange(NX)
    gathered = 8 * (row % 16) + row // 16
    row = np.arange(6 * 32)
    spread = (8 * (row % 16) + 4 * (row // 16 % 2) + row // 32 - 1) % NX
    return {
        "x_in": halves(cas_x[:, gathered]),
        "x_spread": halves(cas_x[spread, :]),
        "x": halves(cas_x),
        "y": halves(cas_y),
        "z": halves(cas_z),
        "symbol": np.asarray(symbol_row(NX)[:, None] + symbol_row(NY)[None, :], np.float32),
    }


def shift_of(frequency):
    phase = 2.0 * math.pi * frequency / STEPS
    return (1.0 - ROOT * math.cos(phase), ROOT * math.sin(phase) if frequency % 4 else 0.0)


def split(value):
    high = value.astype(bf16)
    return high, (value - high.astype(f32)).astype(bf16)


def dot(left, right):
    return jnp.dot(left, right, preferred_element_type=f32)


def left_mul(table_ref, value):
    high, low = split(value)
    return dot(table_ref[0], high) + (dot(table_ref[0], low) + dot(table_ref[1], high))


def right_mul(value, table_ref):
    high, low = split(value)
    return dot(high, table_ref[0]) + (dot(low, table_ref[0]) + dot(high, table_ref[1]))


def vmem():
    return pl.BlockSpec(memory_space=pltpu.VMEM)


def smem():
    return pl.BlockSpec(memory_space=pltpu.SMEM)


def hbm():
    return pl.BlockSpec(memory_space=pltpu.HBM)


def shape(*dims):
    return jax.ShapeDtypeStruct(dims, f32)


def enter_kernel(
    place_ref, source_hbm, initial_hbm, kappa_hbm, z_hbm, out_ref, source_ref, initial_ref, kappa_ref, z_ref, sems
):
    position = place_ref[0]
    table_copy = pltpu.make_async_copy(z_hbm, z_ref, sems.at[16])
    kappa_copy = pltpu.make_async_copy(kappa_hbm.at[position], kappa_ref, sems.at[17])
    copies = [pltpu.make_async_copy(source_hbm.at[x], source_ref.at[x], sems.at[x]) for x in range(8)]
    added = [pltpu.make_async_copy(initial_hbm.at[x], initial_ref.at[x], sems.at[8 + x]) for x in range(8)]
    table_copy.start()
    for copy in copies:
        copy.start()
    kappa_copy.start()

    @pl.when(position == 0)
    def _():
        for copy in added:
            copy.start()

    table_copy.wait()
    nt = (((1,), (1,)), ((), ()))
    dims = functools.partial(lax.dot_general, dimension_numbers=nt, preferred_element_type=f32)
    for x in range(8):
        copies[x].wait()

        @pl.when(position == 0)
        def _(x=x):
            added[x].wait()
            source_ref[x] = source_ref[x] + initial_ref[x]

        high, low = split(source_ref[x])
        freq = dims(z_ref[0], high) + (dims(z_ref[0], low) + dims(z_ref[1], high))
        for yh in range(2):
            for block in range(16):
                out_ref[pl.ds(block * 8 * 17 + yh * 8 + x, 8, stride=17), :] = freq[
                    block * 8 : block * 8 + 8, yh * 128 : yh * 128 + 128
                ]
    kappa_copy.wait()
    total = jnp.sum(kappa_ref[...].reshape(32, 8, 128), axis=0)
    whole = jnp.broadcast_to(jnp.sum(total, keepdims=True), (8, 128))
    for block in range(16):
        out_ref[pl.ds(block * 8 * 17 + 16, 8, stride=17), :] = whole


def precondition_fields(work, kappa, symbol_z, symbol_ref, out):
    symbol = symbol_ref[...] + symbol_z
    scaled = step_length * kappa * symbol
    for pair in range(4):
        first = work[pl.ds(pair * 256, 128), :]
        second = work[pl.ds(pair * 256 + 128, 128), :]
        if pair == 0:
            out[pl.ds(0, 128), :] = first / (shift_of(0)[0] + scaled)
            out[pl.ds(128, 128), :] = second / (shift_of(4)[0] + scaled)
        else:
            shift = shift_of(pair)
            denom = shift[0] + scaled
            inverse = 1.0 / (denom * denom + shift[1] * shift[1])
            real, imag = denom * inverse, shift[1] * inverse
            out[pl.ds(pair * 256, 128), :] = first * real + second * imag
            out[pl.ds(pair * 256 + 128, 128), :] = second * real - first * imag


def spectral_core(
    kappa, symbol_z, gathered, x_in_ref, x_spread_ref, y_ref, symbol_ref, hat_ref, out_ref, work, keep=None
):
    for field in range(8):
        work[pl.ds(field * 128, 128), :] = left_mul(x_in_ref, gathered[pl.ds(field * 128, 128), :])
    work[...] = right_mul(work[...], y_ref)
    precondition_fields(work, kappa, symbol_z, symbol_ref, hat_ref)
    if keep is not None:
        keep.start()
    work[...] = right_mul(hat_ref[...], y_ref)
    for field in range(8):
        spread = left_mul(x_spread_ref, work[pl.ds(field * 128, 128), :])
        pair, part = field // 2, field % 2
        for x in range(6):
            for core in range(2):
                for block in range(2):
                    row = (x * 2 + core) * 16 + block * 8
                    base = ((2 * pair + core) * 16 + block * 8) * 24 + part * 6 + x
                    for yh in range(2):
                        out_ref[pl.ds(base + yh * 12, 8, stride=24), :] = spread[
                            row : row + 8, yh * 128 : yh * 128 + 128
                        ]


def spectral_first_kernel(
    symbol_z_ref,
    in_ref,
    x_in_ref,
    x_spread_ref,
    y_ref,
    symbol_ref,
    hat_hbm,
    out_ref,
    kappa_ref,
    gathered,
    work,
    hat_ref,
    sem,
):
    parts = in_ref[pl.ds(16, 8, stride=17), :]
    for block in range(1, 16):
        parts = parts + in_ref[pl.ds(16 + block * 8 * 17, 8, stride=17), :]
    kappa = jnp.sum(parts, axis=0, keepdims=True) * (1.0 / (NX * NY * NZ))
    kappa_ref[...] = jnp.broadcast_to(kappa, (8, 128))
    kappa = kappa[:, 0:1]
    for x in range(8):
        for block in range(2):
            for yh in range(2):
                lifted = []
                for step in range(8):
                    row = (step * 16 + block * 8) * 17 + yh * 8 + x
                    lifted.append(in_ref[pl.ds(row, 8, stride=17), :] * (alpha_corner ** (step / STEPS)))
                plus = [lifted[m] + lifted[m + 4] for m in range(4)]
                minus = [lifted[m] - lifted[m + 4] for m in range(4)]
                odd_minus = HALF * (minus[1] - minus[3])
                odd_plus = HALF * (minus[1] + minus[3])
                even, odd = plus[0] + plus[2], plus[1] + plus[3]
                fields = [
                    even + odd,
                    even - odd,
                    minus[0] + odd_minus,
                    -minus[2] - odd_plus,
                    plus[0] - plus[2],
                    plus[3] - plus[1],
                    minus[0] - odd_minus,
                    minus[2] - odd_plus,
                ]
                for field in range(8):
                    gathered[pl.ds(field * 128 + x * 16 + block * 8, 8), pl.ds(yh * 128, 128)] = fields[field]
    keep = pltpu.make_async_copy(hat_ref, hat_hbm, sem)
    spectral_core(
        kappa, symbol_z_ref[0], gathered, x_in_ref, x_spread_ref, y_ref, symbol_ref, hat_ref, out_ref, work, keep
    )
    keep.wait()


def spectral_second_kernel(
    symbol_z_ref, kappa_ref, in_ref, x_in_ref, x_spread_ref, y_ref, symbol_ref, hat_ref, out_ref, gathered, work
):
    for field in range(8):
        pair, part = field // 2, field % 2
        for core in range(2):
            for x in range(4):
                for block in range(2):
                    for yh in range(2):
                        row = ((2 * pair + core) * 16 + block * 8) * 16 + yh * 8 + part * 4 + x
                        gathered[
                            pl.ds(field * 128 + (core * 4 + x) * 16 + block * 8, 8), pl.ds(yh * 128, 128)
                        ] = in_ref[pl.ds(row, 8, stride=16), :]
    kappa = kappa_ref[0:1, 0:1]
    spectral_core(
        kappa, symbol_z_ref[0], gathered, x_in_ref, x_spread_ref, y_ref, symbol_ref, hat_ref, out_ref, work
    )


def coefficients(sums):
    lane = lax.broadcasted_iota(jnp.int32, (4, 128), 1)

    def pick(number):
        return jnp.sum(jnp.where(lane == number, sums, 0.0), axis=1, keepdims=True)

    values = [pick(number) for number in range(16)]
    packed = lax.broadcasted_iota(jnp.int32, (4, 1), 0) == 0

    def complex_of(base):
        return values[base] + values[base + 1], values[base + 2] - values[base + 3]

    def solve(g11, g22, g12, h1, h2):
        scale1 = jnp.where(g11 > 0.0, lax.rsqrt(jnp.maximum(g11, 1e-37)), 0.0)
        scale2 = jnp.where(g22 > 0.0, lax.rsqrt(jnp.maximum(g22, 1e-37)), 0.0)
        corr = (g12[0] * scale1 * scale2, g12[1] * scale1 * scale2)
        t1 = (h1[0] * scale1, h1[1] * scale1)
        t2 = (h2[0] * scale2, h2[1] * scale2)
        det = 1.0 - (corr[0] * corr[0] + corr[1] * corr[1])
        good = jnp.logical_and(det > 1e-6, g22 > 0.0)
        inv = jnp.where(good, 1.0 / jnp.where(good, det, 1.0), 0.0)
        one = (
            jnp.where(good, (t1[0] - (corr[0] * t2[0] - corr[1] * t2[1])) * inv, t1[0]),
            jnp.where(good, (t1[1] - (corr[0] * t2[1] + corr[1] * t2[0])) * inv, t1[1]),
        )
        two = (
            (t2[0] - (corr[0] * t1[0] + corr[1] * t1[1])) * inv,
            (t2[1] - (corr[0] * t1[1] - corr[1] * t1[0])) * inv,
        )
        return (1.0 - one[0] * scale1, -one[1] * scale1), (-two[0] * scale2, -two[1] * scale2)

    zero = jnp.zeros((4, 1), f32)
    full = solve(values[0] + values[1], values[2] + values[3], complex_of(4), complex_of(8), complex_of(12))
    first = solve(values[0], values[2], (values[4], zero), (values[8], zero), (values[12], zero))
    second = solve(values[1], values[3], (values[5], zero), (values[9], zero), (values[13], zero))
    maps = []
    for vector in range(2):
        maps.append(
            (
                jnp.where(packed, first[vector][0], full[vector][0]),
                jnp.where(packed, 0.0, full[vector][1]),
                jnp.where(packed, second[vector][0], full[vector][0]),
            )
        )
    return maps


def spectral_last_kernel(sums_ref, hat_one_ref, hat_two_ref, x_ref, y_ref, out_ref, work):
    sums = jnp.concatenate(
        [jnp.sum(sums_ref[pl.ds(pair * 32, 32), :], axis=0, keepdims=True) for pair in range(4)], axis=0
    )
    maps = coefficients(sums)
    scales = [[[entry[pair : pair + 1, :] for entry in vector] for pair in range(4)] for vector in maps]
    for block in range(16):
        rows = 8
        fields = []
        for pair in range(4):
            parts = []
            for hat in (hat_one_ref, hat_two_ref):
                parts.append(
                    (
                        hat[pl.ds(pair * 256 + block * rows, rows), :],
                        hat[pl.ds(pair * 256 + 128 + block * rows, rows), :],
                    )
                )
            (p1, q1), (p2, q2) = parts
            (a1, b1, c1), (a2, b2, c2) = scales[0][pair], scales[1][pair]
            fields.append(a1 * p1 - b1 * q1 + (a2 * p2 - b2 * q2))
            fields.append(c1 * q1 + b1 * p1 + (c2 * q2 + b2 * p2))
        zero, four, re1, im1, re2, im2, re3, im3 = fields
        even = [zero + four + 2.0 * re2, zero - four - 2.0 * im2, zero + four - 2.0 * re2, zero - four + 2.0 * im2]
        diff, total = (2.0 * HALF) * (re1 - re3), (2.0 * HALF) * (im1 + im3)
        odd = [2.0 * (re1 + re3), diff - total, 2.0 * (im3 - im1), -diff - total]
        for step in range(8):
            value = even[step % 4] + odd[step % 4] if step < 4 else even[step % 4] - odd[step % 4]
            scale = alpha_corner ** (-step / STEPS) / STEPS
            work[pl.ds(step * 128 + block * rows, rows), :] = value * scale
    work[...] = right_mul(work[...], y_ref)
    for step in range(8):
        planes = left_mul(x_ref, work[pl.ds(step * 128, 128), :])
        for slab in range(16):
            for yh in range(2):
                out_ref[pl.ds((step * 16 + slab) * 16 + yh * 8, 8), :] = planes[
                    slab * 8 : slab * 8 + 8, yh * 128 : yh * 128 + 128
                ]


def planes_kernel(place_ref, kappa_ref, rim_ref, planes_ref):
    core = lax.rem(place_ref[0], 2)
    rim = rim_ref[0]
    for x in range(6):
        if x == 0:
            plane = jnp.where(core == 0, rim, kappa_ref[3])
        elif x == 5:
            plane = jnp.where(core == 0, kappa_ref[4], rim)
        else:
            plane = kappa_ref[4 * core + x - 1]
        planes_ref[x] = plane.T


def load_block(in_ref, z_ref, field):
    for part in range(2):
        for x in range(6):
            columns = []
            for yh in range(2):
                rows = [in_ref[pl.ds(block * 8 * 24 + yh * 12 + part * 6 + x, 8, stride=24), :] for block in range(16)]
                columns.append(jnp.concatenate(rows, axis=0))
            field[part, x] = left_mul(z_ref, jnp.concatenate(columns, axis=1))


def faces_of(planes_ref, x, kappa):
    plane = planes_ref[x + 1]
    return (
        0.5 * (planes_ref[x] + plane) - kappa,
        0.5 * (plane + planes_ref[x + 2]) - kappa,
        0.5 * (plane + pltpu.roll(plane, NY - 1, 1)) - kappa,
        0.5 * (plane + pltpu.roll(plane, NZ - 1, 0)) - kappa,
    )


def difference(field, part, x, faces):
    here = field[part, x + 1]
    flux_low = faces[0] * (here - field[part, x])
    flux_high = faces[1] * (field[part, x + 2] - here)
    flux_y = faces[2] * (pltpu.roll(here, NY - 1, 1) - here)
    flux_z = faces[3] * (pltpu.roll(here, NZ - 1, 0) - here)
    return (
        (flux_low - flux_high) + (pltpu.roll(flux_y, 1, 1) - flux_y) + (pltpu.roll(flux_z, 1, 0) - flux_z)
    )


def constant_part(field, part, x):
    here = field[part, x + 1]
    around = field[part, x] + field[part, x + 2]
    around = around + pltpu.roll(here, NY - 1, 1) + pltpu.roll(here, 1, 1)
    around = around + pltpu.roll(here, NZ - 1, 0) + pltpu.roll(here, 1, 0)
    return 6.0 * here - around


def block_first_kernel(
    place_ref, kappa_ref, in_ref, z_ref, planes_ref, out_ref, differ_ref, right_ref, field
):
    kappa = kappa_ref[0:1, 0:1]
    pair = place_ref[0] // 2
    real = [jnp.float32(shift_of(4 * part)[0]) for part in range(2)]
    imag = jnp.float32(0.0)
    for number in range(1, 4):
        real = [jnp.where(pair == number, shift_of(number)[0], value) for value in real]
        imag = jnp.where(pair == number, shift_of(number)[1], imag)
    load_block(in_ref, z_ref, field)
    for x in range(4):
        faces = faces_of(planes_ref, x, kappa)
        for part in range(2):
            value = difference(field, part, x, faces)
            differ_ref[part, x] = value
            freq = left_mul(z_ref, value)
            for yh in range(2):
                for block in range(16):
                    out_ref[pl.ds(block * 8 * 16 + yh * 8 + part * 4 + x, 8, stride=16), :] = freq[
                        block * 8 : block * 8 + 8, yh * 128 : yh * 128 + 128
                    ]
            here, other = field[part, x + 1], field[1 - part, x + 1]
            cross = -imag if part == 0 else imag
            right_ref[part, x] = (
                real[part] * here + cross * other + (step_length * kappa) * constant_part(field, part, x)
            )


def block_second_kernel(
    kappa_ref, in_ref, differ_ref, right_ref, z_ref, planes_ref, out_ref, field
):
    kappa = kappa_ref[0:1, 0:1]
    load_block(in_ref, z_ref, field)
    totals = [jnp.zeros((8, 256), f32) for _ in range(16)]

    def fold(value):
        return jnp.sum(value.reshape(16, 8, 256), axis=0)

    for x in range(4):
        faces = faces_of(planes_ref, x, kappa)
        diffs = [differ_ref[part, x] for part in range(2)]
        ones = [right_ref[part, x] + diffs[part] for part in range(2)]
        twos = [diffs[part] + difference(field, part, x, faces) for part in range(2)]
        pairs = [(ones[0], ones[0]), (ones[1], ones[1]), (twos[0], twos[0]), (twos[1], twos[1])]
        for left, right in ((ones, twos), (ones, diffs), (twos, diffs)):
            pairs += [(left[0], right[0]), (left[1], right[1]), (left[0], right[1]), (left[1], right[0])]
        for number, (left, right) in enumerate(pairs):
            totals[number] = totals[number] + fold(left * right)
    lane = lax.broadcasted_iota(jnp.int32, (1, 128), 1)
    row = jnp.zeros((1, 128), f32)
    for number in range(16):
        row = row + jnp.where(lane == number, jnp.sum(totals[number], keepdims=True), 0.0)
    out_ref[...] = jnp.broadcast_to(row, (DEVS, 128))


def leave_kernel(in_ref, z_ref, out_hbm, out_ref, sems):
    copies = [pltpu.make_async_copy(out_ref.at[x], out_hbm.at[0, x], sems.at[x]) for x in range(8)]
    for x in range(8):
        columns = []
        for yh in range(2):
            rows = [in_ref[pl.ds(block * 8 * 16 + yh * 8 + x, 8, stride=16), :] for block in range(16)]
            columns.append(jnp.concatenate(rows, axis=0))
        value = left_mul(z_ref, jnp.concatenate(columns, axis=1))
        out_ref[x] = value.T
        copies[x].start()
    for copy in copies:
        copy.wait()


def exchange(rows):
    wide = rows.reshape(rows.shape[0], 1, 128)
    return lax.all_to_all(wide, BOTH, split_axis=0, concat_axis=0, tiled=True).reshape(rows.shape)


def call(kernel, outs, scalars, scratch, *args, far_in=(), far_out=()):
    args = [
        pltpu.with_memory_space_constraint(arg, pltpu.HBM) if number in far_in else arg
        for number, arg in enumerate(args)
    ]
    outs = [
        pltpu.HBM(out.shape, out.dtype) if number in far_out else out for number, out in enumerate(outs)
    ]
    return pl.pallas_call(
        kernel,
        out_shape=outs,
        in_specs=[
            smem() if number < scalars else (hbm() if number in far_in else vmem()) for number in range(len(args))
        ],
        out_specs=[hbm() if number in far_out else vmem() for number in range(len(outs))],
        scratch_shapes=scratch,
        name=kernel.__name__,
        compiler_params=pltpu.CompilerParams(vmem_limit_bytes=24 << 20),
    )(*args)


def shards(source, initial, diffusivity):
    table = tables()
    position = lax.axis_index("tm")
    slab = lax.axis_index("space")
    wave = (position * SLABS + slab).astype(f32)
    symbol_z = (4.0 * jnp.sin(math.pi * wave / NZ) ** 2).reshape(1)
    core_is_low = position % 2 == 0
    place = position.astype(jnp.int32).reshape(1)
    source, place, symbol_z, core_is_low = lax.optimization_barrier((source, place, symbol_z, core_is_low))

    rim_out = jnp.where(core_is_low, diffusivity[7], diffusivity[0])[None]
    route = []
    for time in range(STEPS):
        for node in range(SLABS):
            step = 1 if time % 2 == 0 else SLABS - 1
            route.append((time * SLABS + node, time * SLABS + (node + step) % SLABS))
    rim = lax.ppermute(rim_out, BOTH, route)
    (planes,) = call(planes_kernel, [shape(6, NZ, NY)], 1, [], place, diffusivity, rim)

    slab_block = pltpu.VMEM((8, NY, NZ), f32)
    (rows,) = call(
        enter_kernel,
        [shape(DEVS * 17, 128)],
        1,
        [
            slab_block,
            slab_block,
            pltpu.VMEM((NY, NZ), f32),
            pltpu.VMEM((2, NZ, NZ), bf16),
            pltpu.SemaphoreType.DMA((18,)),
        ],
        place,
        source[0],
        initial,
        diffusivity,
        table["z"],
        far_in=(1, 2, 3, 4),
    )
    rows, planes = lax.optimization_barrier((exchange(rows), planes))
    big = pltpu.VMEM((1024, NY), f32)
    hat_one, rows, kappa = call(
        spectral_first_kernel,
        [shape(1024, NY), shape(DEVS * 24, 128), shape(8, 128)],
        1,
        [big, big, big, pltpu.SemaphoreType.DMA],
        symbol_z,
        rows,
        table["x_in"],
        table["x_spread"],
        table["y"],
        table["symbol"],
        far_out=(0,),
    )
    rows = exchange(rows)
    block = pltpu.VMEM((2, 6, NZ, NY), f32)
    rows, differ, right = call(
        block_first_kernel,
        [shape(DEVS * 16, 128), shape(2, 4, NZ, NY), shape(2, 4, NZ, NY)],
        1,
        [block],
        place,
        kappa,
        rows,
        table["z"],
        planes,
    )
    rows = exchange(rows)
    hat_two, rows = call(
        spectral_second_kernel,
        [shape(1024, NY), shape(DEVS * 24, 128)],
        1,
        [big, big],
        symbol_z,
        kappa,
        rows,
        table["x_in"],
        table["x_spread"],
        table["y"],
        table["symbol"],
    )
    rows = exchange(rows)
    (sums,) = call(block_second_kernel, [shape(DEVS, 128)], 0, [block], kappa, rows, differ, right, table["z"], planes)
    sums = exchange(sums)
    (rows,) = call(
        spectral_last_kernel, [shape(DEVS * 16, 128)], 0, [big], sums, hat_one, hat_two, table["x"], table["y"]
    )
    rows = exchange(rows)
    (field,) = call(
        leave_kernel,
        [shape(1, 8, NY, NZ)],
        0,
        [slab_block, pltpu.SemaphoreType.DMA((8,))],
        rows,
        table["z"],
        far_out=(0,),
    )
    return field


def solution(mesh):
    in_specs = (P("tm", "space", None, None), P("space", None, None), P("space", None, None))
    out_specs = P("tm", "space", None, None)
    return jax.shard_map(shards, mesh=mesh, in_specs=in_specs, out_specs=out_specs, check_vma=False)
```

```python
import functools
import math

import jax
import jax.numpy as jnp
import numpy as np
from jax import lax
from jax.experimental import pallas as pl
from jax.experimental.pallas import tpu as pltpu
from jax.sharding import PartitionSpec as P


alpha_corner = 0.05
step_length = 1.0
BOTH = ("tm", "space")
NX, NY, NZ = 128, 256, 128
STEPS = 8
ROWS = 21
ROWS_FIRST = 23
SLABS = 16
DEVS = 128
f32 = jnp.float32
bf16 = jnp.bfloat16
ROOT = alpha_corner ** (1.0 / STEPS)
HALF = math.sqrt(0.5)


def cas_table(length):
    index = np.arange(length)
    phase = (index[:, None] * index[None, :] % length) * (2.0 * np.pi / length)
    return (np.cos(phase) + np.sin(phase)) / math.sqrt(length)


def halves(table):
    table = np.asarray(table, np.float32)
    high = table.astype(bf16)
    low = (table - high.astype(np.float32)).astype(bf16)
    return np.stack([high, low])


def symbol_row(length):
    return 4.0 * np.sin(np.pi * np.arange(length) / length) ** 2


def tables():
    cas_x, cas_y, cas_z = cas_table(NX), cas_table(NY), cas_table(NZ)
    row = np.arange(NX)
    gathered = 8 * (row % 16) + row // 16
    row = np.arange(10 * 16)
    spread = (8 * (row % 16) + row // 16 - 1) % NX
    x_in, x_spread, y = halves(cas_x[:, gathered]), halves(cas_x[spread, :]), halves(cas_y)
    y_rows = [y[part, :, half * 128 : half * 128 + 128] for part in range(2) for half in range(2)]
    return {
        "spectral": np.concatenate([x_in[0], x_in[1], x_spread[0], x_spread[1], *y_rows]),
        "x": halves(cas_x),
        "y": y,
        "z": halves(cas_z),
        "symbol": np.asarray(symbol_row(NX)[:, None] + symbol_row(NY)[None, :], np.float32),
    }


def shift_of(frequency):
    phase = 2.0 * math.pi * frequency / STEPS
    return (1.0 - ROOT * math.cos(phase), ROOT * math.sin(phase) if frequency % 4 else 0.0)


def split(value):
    high = value.astype(bf16)
    return high, (value - high.astype(f32)).astype(bf16)


def dot(left, right):
    return jnp.dot(left, right, preferred_element_type=f32)


def left_mul(table, value):
    high, low = split(value)
    return dot(table[0], high) + (dot(table[0], low) + dot(table[1], high))


def right_mul(value, table):
    high, low = split(value)
    return dot(high, table[0]) + (dot(low, table[0]) + dot(high, table[1]))


def spectral_parts(table_ref):
    x_in = table_ref[0:128, :], table_ref[128:256, :]
    x_spread = table_ref[256:416, :], table_ref[416:576, :]
    y = [
        jnp.concatenate([table_ref[row : row + 256, :], table_ref[row + 256 : row + 512, :]], axis=1)
        for row in (576, 1088)
    ]
    return x_in, x_spread, y


def vmem():
    return pl.BlockSpec(memory_space=pltpu.VMEM)


def smem():
    return pl.BlockSpec(memory_space=pltpu.SMEM)


def hbm():
    return pl.BlockSpec(memory_space=pltpu.HBM)


def shape(*dims):
    return jax.ShapeDtypeStruct(dims, f32)


def enter_kernel(
    place_ref,
    source_hbm,
    initial_hbm,
    kappa_hbm,
    z_hbm,
    out_ref,
    source_ref,
    initial_ref,
    kappa_ref,
    rim_ref,
    z_ref,
    sems,
):
    position = place_ref[0]
    first = jnp.where(position == 0, jnp.float32(1.0), jnp.float32(0.0))
    quarter = lax.rem(position, 4)
    half = pl.ds(pl.multiple_of(lax.rem(position, 2) * 128, 128), 128)
    table_copy = pltpu.make_async_copy(z_hbm, z_ref, sems.at[16])
    kappa_copy = pltpu.make_async_copy(kappa_hbm.at[pl.ds(2 * quarter, 2)], kappa_ref, sems.at[17])
    rim_copy = pltpu.make_async_copy(kappa_hbm.at[7 * (quarter // 2), half], rim_ref, sems.at[18])
    copies = [pltpu.make_async_copy(source_hbm.at[x], source_ref.at[x], sems.at[x]) for x in range(8)]
    added = [pltpu.make_async_copy(initial_hbm.at[x], initial_ref.at[x], sems.at[8 + x]) for x in range(8)]
    table_copy.start()
    for x in range(8):
        copies[x].start()
        added[x].start()
    kappa_copy.start()
    rim_copy.start()
    table_copy.wait()
    nt = (((1,), (1,)), ((), ()))
    dims = functools.partial(lax.dot_general, dimension_numbers=nt, preferred_element_type=f32)
    for x in range(8):
        copies[x].wait()
        added[x].wait()
        high, low = split(source_ref[x] + first * initial_ref[x])
        freq = dims(z_ref[0], high) + (dims(z_ref[0], low) + dims(z_ref[1], high))
        for yh in range(2):
            for block in range(16):
                out_ref[pl.ds(block * 8 * 17 + yh * 8 + x, 8, stride=17), :] = freq[
                    block * 8 : block * 8 + 8, yh * 128 : yh * 128 + 128
                ]
    kappa_copy.wait()
    rim_copy.wait()
    total = jnp.sum(kappa_ref[...].reshape(64, 8, 128), axis=0)
    whole = jnp.broadcast_to(jnp.sum(total, keepdims=True), (8, 128))
    rim = rim_ref[...].T
    for block in range(16):
        out_ref[pl.ds(block * 8 * 17 + 16, 8, stride=17), :] = jnp.where(
            position < 4, rim[block * 8 : block * 8 + 8], whole
        )


def precondition_fields(work, kappa, symbol_z, symbol_ref, out):
    symbol = symbol_ref[...] + symbol_z
    scaled = step_length * kappa * symbol
    for pair in range(4):
        first = work[pl.ds(pair * 256, 128), :]
        second = work[pl.ds(pair * 256 + 128, 128), :]
        if pair == 0:
            out[pl.ds(0, 128), :] = first / (shift_of(0)[0] + scaled)
            out[pl.ds(128, 128), :] = second / (shift_of(4)[0] + scaled)
        else:
            shift = shift_of(pair)
            denom = shift[0] + scaled
            inverse = 1.0 / (denom * denom + shift[1] * shift[1])
            real, imag = denom * inverse, shift[1] * inverse
            out[pl.ds(pair * 256, 128), :] = first * real + second * imag
            out[pl.ds(pair * 256 + 128, 128), :] = second * real - first * imag


def spectral_core(
    kappa, symbol_z, gathered, table_ref, symbol_ref, hat_ref, out_ref, work, count, keep=None
):
    x_in_ref, x_spread_ref, y_ref = spectral_parts(table_ref)
    for field in range(8):
        work[pl.ds(field * 128, 128), :] = left_mul(x_in_ref, gathered[pl.ds(field * 128, 128), :])
    work[...] = right_mul(work[...], y_ref)
    precondition_fields(work, kappa, symbol_z, symbol_ref, hat_ref)
    if keep is not None:
        keep.start()
    work[...] = right_mul(hat_ref[...], y_ref)
    lane = lax.broadcasted_iota(jnp.int32, (8, 128), 1)
    for pair in range(4):
        edges = {}
        for part in range(2):
            spread = left_mul(x_spread_ref, work[pl.ds((pair * 2 + part) * 128, 128), :])
            for core in range(2):
                for block in range(2):
                    base = ((2 * pair + core) * 16 + block * 8) * count
                    edge = edges.get((core, block), jnp.zeros((8, 128), f32))
                    for x in range(10):
                        rows = spread[x * 16 + block * 8 : x * 16 + block * 8 + 8]
                        out_ref[pl.ds(base + part * 10 + x, 8, stride=count), :] = rows[:, core * 128 : core * 128 + 128]
                        if 1 <= x <= 8:
                            spot = 2 * (part * 8 + x - 1)
                            other = rows[:, (1 - core) * 128 : (1 - core) * 128 + 128]
                            edge = jnp.where(lane // 2 == spot // 2, pltpu.roll(other, spot + 1, 1), edge)
                    edges[core, block] = edge
        for core in range(2):
            for block in range(2):
                base = ((2 * pair + core) * 16 + block * 8) * count
                out_ref[pl.ds(base + 20, 8, stride=count), :] = edges[core, block]


def spectral_first_kernel(
    symbol_z_ref,
    in_ref,
    table_ref,
    symbol_ref,
    hat_hbm,
    out_ref,
    kappa_ref,
    gathered,
    work,
    hat_ref,
    sem,
):
    def extra(step, block):
        return in_ref[pl.ds((step * 16 + block * 8) * 17 + 16, 8, stride=17), :]

    row = lax.broadcasted_iota(jnp.int32, (8, 128), 0)
    for core in range(2):
        first, last = [extra(core, 0), extra(core, 1)], [extra(2 + core, 0), extra(2 + core, 1)]
        for block in range(2):
            low = jnp.where(row == 0, pltpu.roll(last[1 - block], 1, 0), pltpu.roll(last[block], 1, 0))
            high = jnp.where(row == 7, pltpu.roll(first[1 - block], 7, 0), pltpu.roll(first[block], 7, 0))
            for pair in range(4):
                base = ((2 * pair + core) * 16 + block * 8) * ROWS_FIRST
                out_ref[pl.ds(base + 21, 8, stride=ROWS_FIRST), :] = low
                out_ref[pl.ds(base + 22, 8, stride=ROWS_FIRST), :] = high
    parts = extra(4, 0) + extra(4, 1)
    for step in range(5, 8):
        parts = parts + (extra(step, 0) + extra(step, 1))
    kappa = jnp.sum(parts, axis=0, keepdims=True) * (1.0 / (NX * NY * NZ))
    kappa_ref[...] = jnp.broadcast_to(kappa, (8, 128))
    kappa = kappa[:, 0:1]
    for x in range(8):
        for block in range(2):
            for yh in range(2):
                lifted = []
                for step in range(8):
                    row = (step * 16 + block * 8) * 17 + yh * 8 + x
                    lifted.append(in_ref[pl.ds(row, 8, stride=17), :] * (alpha_corner ** (step / STEPS)))
                plus = [lifted[m] + lifted[m + 4] for m in range(4)]
                minus = [lifted[m] - lifted[m + 4] for m in range(4)]
                odd_minus = HALF * (minus[1] - minus[3])
                odd_plus = HALF * (minus[1] + minus[3])
                even, odd = plus[0] + plus[2], plus[1] + plus[3]
                fields = [
                    even + odd,
                    even - odd,
                    minus[0] + odd_minus,
                    -minus[2] - odd_plus,
                    plus[0] - plus[2],
                    plus[3] - plus[1],
                    minus[0] - odd_minus,
                    minus[2] - odd_plus,
                ]
                for field in range(8):
                    gathered[pl.ds(field * 128 + x * 16 + block * 8, 8), pl.ds(yh * 128, 128)] = fields[field]
    keep = pltpu.make_async_copy(hat_ref, hat_hbm, sem)
    spectral_core(
        kappa, symbol_z_ref[0], gathered, table_ref, symbol_ref, hat_ref, out_ref, work, ROWS_FIRST, keep
    )
    keep.wait()


def spectral_second_kernel(
    symbol_z_ref, kappa_ref, in_ref, table_ref, symbol_ref, hat_ref, out_ref, gathered, work
):
    for field in range(8):
        pair, part = field // 2, field % 2
        for core in range(2):
            for x in range(8):
                for block in range(2):
                    row = ((2 * pair + core) * 16 + block * 8) * 16 + part * 8 + x
                    gathered[pl.ds(field * 128 + x * 16 + block * 8, 8), pl.ds(core * 128, 128)] = in_ref[
                        pl.ds(row, 8, stride=16), :
                    ]
    kappa = kappa_ref[0:1, 0:1]
    spectral_core(
        kappa, symbol_z_ref[0], gathered, table_ref, symbol_ref, hat_ref, out_ref, work, ROWS
    )


def coefficients(sums):
    lane = lax.broadcasted_iota(jnp.int32, (4, 128), 1)

    def pick(number):
        return jnp.sum(jnp.where(lane == number, sums, 0.0), axis=1, keepdims=True)

    values = [pick(number) for number in range(16)]
    packed = lax.broadcasted_iota(jnp.int32, (4, 1), 0) == 0

    def complex_of(base):
        return values[base] + values[base + 1], values[base + 2] - values[base + 3]

    def solve(g11, g22, g12, h1, h2):
        scale1 = jnp.where(g11 > 0.0, lax.rsqrt(jnp.maximum(g11, 1e-37)), 0.0)
        scale2 = jnp.where(g22 > 0.0, lax.rsqrt(jnp.maximum(g22, 1e-37)), 0.0)
        corr = (g12[0] * scale1 * scale2, g12[1] * scale1 * scale2)
        t1 = (h1[0] * scale1, h1[1] * scale1)
        t2 = (h2[0] * scale2, h2[1] * scale2)
        det = 1.0 - (corr[0] * corr[0] + corr[1] * corr[1])
        good = jnp.logical_and(det > 1e-6, g22 > 0.0)
        inv = jnp.where(good, 1.0 / jnp.where(good, det, 1.0), 0.0)
        one = (
            jnp.where(good, (t1[0] - (corr[0] * t2[0] - corr[1] * t2[1])) * inv, t1[0]),
            jnp.where(good, (t1[1] - (corr[0] * t2[1] + corr[1] * t2[0])) * inv, t1[1]),
        )
        two = (
            (t2[0] - (corr[0] * t1[0] + corr[1] * t1[1])) * inv,
            (t2[1] - (corr[0] * t1[1] - corr[1] * t1[0])) * inv,
        )
        return (1.0 - one[0] * scale1, -one[1] * scale1), (-two[0] * scale2, -two[1] * scale2)

    zero = jnp.zeros((4, 1), f32)
    full = solve(values[0] + values[1], values[2] + values[3], complex_of(4), complex_of(8), complex_of(12))
    first = solve(values[0], values[2], (values[4], zero), (values[8], zero), (values[12], zero))
    second = solve(values[1], values[3], (values[5], zero), (values[9], zero), (values[13], zero))
    maps = []
    for vector in range(2):
        maps.append(
            (
                jnp.where(packed, first[vector][0], full[vector][0]),
                jnp.where(packed, 0.0, full[vector][1]),
                jnp.where(packed, second[vector][0], full[vector][0]),
            )
        )
    return maps


def spectral_last_kernel(sums_ref, hat_one_ref, hat_two_ref, x_ref, y_ref, out_ref, work):
    sums = jnp.concatenate(
        [jnp.sum(sums_ref[pl.ds(pair * 32, 32), :], axis=0, keepdims=True) for pair in range(4)], axis=0
    )
    maps = coefficients(sums)
    scales = [[[entry[pair : pair + 1, :] for entry in vector] for pair in range(4)] for vector in maps]
    for block in range(16):
        rows = 8
        fields = []
        for pair in range(4):
            parts = []
            for hat in (hat_one_ref, hat_two_ref):
                parts.append(
                    (
                        hat[pl.ds(pair * 256 + block * rows, rows), :],
                        hat[pl.ds(pair * 256 + 128 + block * rows, rows), :],
                    )
                )
            (p1, q1), (p2, q2) = parts
            (a1, b1, c1), (a2, b2, c2) = scales[0][pair], scales[1][pair]
            fields.append(a1 * p1 - b1 * q1 + (a2 * p2 - b2 * q2))
            fields.append(c1 * q1 + b1 * p1 + (c2 * q2 + b2 * p2))
        zero, four, re1, im1, re2, im2, re3, im3 = fields
        even = [zero + four + 2.0 * re2, zero - four - 2.0 * im2, zero + four - 2.0 * re2, zero - four + 2.0 * im2]
        diff, total = (2.0 * HALF) * (re1 - re3), (2.0 * HALF) * (im1 + im3)
        odd = [2.0 * (re1 + re3), diff - total, 2.0 * (im3 - im1), -diff - total]
        for step in range(8):
            value = even[step % 4] + odd[step % 4] if step < 4 else even[step % 4] - odd[step % 4]
            scale = alpha_corner ** (-step / STEPS) / STEPS
            work[pl.ds(step * 128 + block * rows, rows), :] = value * scale
    work[...] = right_mul(work[...], y_ref)
    for step in range(8):
        planes = left_mul(x_ref, work[pl.ds(step * 128, 128), :])
        for slab in range(16):
            for yh in range(2):
                out_ref[pl.ds((step * 16 + slab) * 16 + yh * 8, 8), :] = planes[
                    slab * 8 : slab * 8 + 8, yh * 128 : yh * 128 + 128
                ]


def faces_kernel(place_ref, kappa_ref, faces_ref):
    upper = lax.rem(place_ref[0], 2) == 1

    def half(plane):
        return jnp.where(upper, plane[128:], plane[:128]).T

    before = None
    for x in range(8):
        whole = kappa_ref[x]
        here = half(whole)
        faces_ref[9 + x] = 0.5 * (here + half(pltpu.roll(whole, NY - 1, 0)))
        faces_ref[17 + x] = 0.5 * (here + half(pltpu.roll(whole, 1, 0)))
        faces_ref[25 + x] = 0.5 * (here + pltpu.roll(here, NZ - 1, 0))
        if x == 0:
            faces_ref[0] = here
        else:
            faces_ref[x] = 0.5 * (before + here)
        before = here
    faces_ref[8] = before


def column(in_ref, number, count):
    return jnp.concatenate(
        [in_ref[pl.ds(block * 8 * count + number, 8, stride=count), :] for block in range(16)], axis=0
    )


def load_block(in_ref, z_ref, field, count):
    for number in range(0, 20, 2):
        columns = [column(in_ref, number + step, count) for step in range(2)]
        both = left_mul(z_ref, jnp.concatenate(columns, axis=1))
        field[number] = both[:, :128]
        field[number + 1] = both[:, 128:]
    field[20] = left_mul(z_ref, column(in_ref, 20, count))


def beside(field, part, x, lane):
    here = field[part * 10 + x + 1]
    spot = 2 * (part * 8 + x)
    edge = field[20]
    below = jnp.where(lane == 0, pltpu.roll(edge, (128 - spot) % 128, 1), pltpu.roll(here, 1, 1))
    above = jnp.where(lane == 127, pltpu.roll(edge, 126 - spot, 1), pltpu.roll(here, 127, 1))
    return here, below, above


def difference(field, part, x, here, below, above, faces_ref, ends, kappa):
    low = ends[0] if x == 0 else faces_ref[x]
    high = ends[1] if x == 7 else faces_ref[x + 1]
    value = (low - kappa) * (here - field[part * 10 + x])
    value = value + (high - kappa) * (here - field[part * 10 + x + 2])
    value = value + (faces_ref[9 + x] - kappa) * (here - above)
    value = value + (faces_ref[17 + x] - kappa) * (here - below)
    flux = (faces_ref[25 + x] - kappa) * (here - pltpu.roll(here, NZ - 1, 0))
    return value + (flux - pltpu.roll(flux, 1, 0))


def constant_part(field, part, x, here, below, above):
    around = (field[part * 10 + x] + field[part * 10 + x + 2]) + (below + above)
    around = around + (pltpu.roll(here, NZ - 1, 0) + pltpu.roll(here, 1, 0))
    return 6.0 * here - around


def block_first_kernel(
    place_ref, kappa_ref, in_ref, z_ref, faces_ref, out_ref, differ_ref, right_ref, ends_ref, field
):
    kappa = kappa_ref[0:1, 0:1]
    pair = place_ref[0] // 2
    real = [jnp.float32(shift_of(4 * part)[0]) for part in range(2)]
    imag = jnp.float32(0.0)
    for number in range(1, 4):
        real = [jnp.where(pair == number, shift_of(number)[0], value) for value in real]
        imag = jnp.where(pair == number, shift_of(number)[1], imag)
    load_block(in_ref, z_ref, field, ROWS_FIRST)
    ends_ref[0] = 0.5 * (column(in_ref, 21, ROWS_FIRST) + faces_ref[0])
    ends_ref[1] = 0.5 * (column(in_ref, 22, ROWS_FIRST) + faces_ref[8])
    lane = lax.broadcasted_iota(jnp.int32, (NZ, 128), 1)
    for x in range(8):
        values = []
        for part in range(2):
            here, below, above = beside(field, part, x, lane)
            value = difference(field, part, x, here, below, above, faces_ref, ends_ref, kappa)
            differ_ref[part, x] = value
            values.append(value)
            other = field[(1 - part) * 10 + x + 1]
            cross = -imag if part == 0 else imag
            right_ref[part, x] = (
                real[part] * here
                + cross * other
                + (step_length * kappa) * constant_part(field, part, x, here, below, above)
            )
        freq = left_mul(z_ref, jnp.concatenate(values, axis=1))
        for part in range(2):
            for block in range(16):
                out_ref[pl.ds(block * 8 * 16 + part * 8 + x, 8, stride=16), :] = freq[
                    block * 8 : block * 8 + 8, part * 128 : part * 128 + 128
                ]


def block_second_kernel(
    kappa_ref, in_ref, differ_ref, right_ref, z_ref, faces_ref, ends_ref, out_ref, field
):
    kappa = kappa_ref[0:1, 0:1]
    load_block(in_ref, z_ref, field, ROWS)
    lane = lax.broadcasted_iota(jnp.int32, (NZ, 128), 1)
    totals = [jnp.zeros((8, 128), f32) for _ in range(16)]

    def fold(value):
        return jnp.sum(value.reshape(16, 8, 128), axis=0)

    for x in range(8):
        diffs = [differ_ref[part, x] for part in range(2)]
        ones = [right_ref[part, x] + diffs[part] for part in range(2)]
        twos = []
        for part in range(2):
            here, below, above = beside(field, part, x, lane)
            twos.append(diffs[part] + difference(field, part, x, here, below, above, faces_ref, ends_ref, kappa))
        pairs = [(ones[0], ones[0]), (ones[1], ones[1]), (twos[0], twos[0]), (twos[1], twos[1])]
        for left, right in ((ones, twos), (ones, diffs), (twos, diffs)):
            pairs += [(left[0], right[0]), (left[1], right[1]), (left[0], right[1]), (left[1], right[0])]
        for number, (left, right) in enumerate(pairs):
            totals[number] = totals[number] + fold(left * right)
    spot = lax.broadcasted_iota(jnp.int32, (1, 128), 1)
    row = jnp.zeros((1, 128), f32)
    for number in range(16):
        row = row + jnp.where(spot == number, jnp.sum(totals[number], keepdims=True), 0.0)
    out_ref[...] = jnp.broadcast_to(row, (DEVS, 128))


def leave_kernel(in_ref, z_ref, out_hbm, out_ref, sems):
    copies = [pltpu.make_async_copy(out_ref.at[x], out_hbm.at[0, x], sems.at[x]) for x in range(8)]
    for x in range(8):
        columns = []
        for yh in range(2):
            rows = [in_ref[pl.ds(block * 8 * 16 + yh * 8 + x, 8, stride=16), :] for block in range(16)]
            columns.append(jnp.concatenate(rows, axis=0))
        value = left_mul(z_ref, jnp.concatenate(columns, axis=1))
        out_ref[x] = value.T
        copies[x].start()
    for copy in copies:
        copy.wait()


def exchange(rows):
    wide = rows.reshape(rows.shape[0], 1, 128)
    return lax.all_to_all(wide, BOTH, split_axis=0, concat_axis=0, tiled=True).reshape(rows.shape)


def call(kernel, outs, scalars, scratch, *args, far_in=(), far_out=(), near_in=(), near_out=()):
    args = [
        pltpu.with_memory_space_constraint(arg, pltpu.HBM) if number in far_in else arg
        for number, arg in enumerate(args)
    ]
    args = [
        pltpu.with_memory_space_constraint(arg, pltpu.VMEM) if number in near_in else arg
        for number, arg in enumerate(args)
    ]
    outs = [pltpu.HBM(out.shape, out.dtype) if number in far_out else out for number, out in enumerate(outs)]
    outs = [pltpu.VMEM(out.shape, out.dtype) if number in near_out else out for number, out in enumerate(outs)]
    return pl.pallas_call(
        kernel,
        out_shape=outs,
        in_specs=[
            smem() if number < scalars else (hbm() if number in far_in else vmem()) for number in range(len(args))
        ],
        out_specs=[hbm() if number in far_out else vmem() for number in range(len(outs))],
        scratch_shapes=scratch,
        name=kernel.__name__,
        compiler_params=pltpu.CompilerParams(vmem_limit_bytes=16 << 20),
    )(*args)


def shards(source, initial, diffusivity):
    table = tables()
    position = lax.axis_index("tm")
    slab = lax.axis_index("space")
    wave = (position * SLABS + slab).astype(f32)
    symbol_z = (4.0 * jnp.sin(math.pi * wave / NZ) ** 2).reshape(1)
    place = position.astype(jnp.int32).reshape(1)
    source, place, symbol_z = lax.optimization_barrier((source, place, symbol_z))

    slab_block = pltpu.VMEM((8, NY, NZ), f32)
    (rows,) = call(
        enter_kernel,
        [shape(DEVS * 17, 128)],
        1,
        [
            slab_block,
            slab_block,
            pltpu.VMEM((2, NY, NZ), f32),
            pltpu.VMEM((128, NZ), f32),
            pltpu.VMEM((2, NZ, NZ), bf16),
            pltpu.SemaphoreType.DMA((19,)),
        ],
        place,
        source[0],
        initial,
        diffusivity,
        table["z"],
        far_in=(1, 2, 3, 4),
    )
    rows, diffusivity = lax.optimization_barrier((exchange(rows), diffusivity))
    (faces,) = call(faces_kernel, [shape(33, NZ, 128)], 1, [], place, diffusivity)
    big = pltpu.VMEM((1024, NY), f32)
    hat_one, rows, kappa = call(
        spectral_first_kernel,
        [shape(1024, NY), shape(DEVS * ROWS_FIRST, 128), shape(8, 128)],
        1,
        [big, big, big, pltpu.SemaphoreType.DMA],
        symbol_z,
        rows,
        table["spectral"],
        table["symbol"],
        far_out=(0,),
        near_in=(1,),
        near_out=(1,),
    )
    rows, faces = lax.optimization_barrier((rows, faces))
    rows = exchange(rows)
    block = pltpu.VMEM((21, NZ, 128), f32)
    rows, differ, right, ends = call(
        block_first_kernel,
        [shape(DEVS * 16, 128), shape(2, 8, NZ, 128), shape(2, 8, NZ, 128), shape(2, NZ, 128)],
        1,
        [block],
        place,
        kappa,
        rows,
        table["z"],
        faces,
    )
    rows = exchange(rows)
    hat_two, rows = call(
        spectral_second_kernel,
        [shape(1024, NY), shape(DEVS * ROWS, 128)],
        1,
        [big, big],
        symbol_z,
        kappa,
        rows,
        table["spectral"],
        table["symbol"],
    )
    rows = exchange(rows)
    (sums,) = call(block_second_kernel, [shape(DEVS, 128)], 0, [block], kappa, rows, differ, right, table["z"], faces, ends)
    sums = exchange(sums)
    (rows,) = call(
        spectral_last_kernel, [shape(DEVS * 16, 128)], 0, [big], sums, hat_one, hat_two, table["x"], table["y"]
    )
    rows = exchange(rows)
    (field,) = call(
        leave_kernel,
        [shape(1, 8, NY, NZ)],
        0,
        [slab_block, pltpu.SemaphoreType.DMA((8,))],
        rows,
        table["z"],
        far_out=(0,),
    )
    return field


def solution(mesh):
    in_specs = (P("tm", "space", None, None), P("space", None, None), P("space", None, None))
    out_specs = P("tm", "space", None, None)
    return jax.shard_map(shards, mesh=mesh, in_specs=in_specs, out_specs=out_specs, check_vma=False)
```

```python
import functools
import math

import jax
import jax.numpy as jnp
import numpy as np
from jax import lax
from jax.experimental import pallas as pl
from jax.experimental.pallas import tpu as pltpu
from jax.sharding import PartitionSpec as P


alpha_corner = 0.05
step_length = 1.0
BOTH = ("tm", "space")
NX, NY, NZ = 128, 256, 128
STEPS = 8
ROWS = 21
ROWS_FIRST = 23
SLABS = 16
DEVS = 128
f32 = jnp.float32
bf16 = jnp.bfloat16
ROOT = alpha_corner ** (1.0 / STEPS)
HALF = math.sqrt(0.5)


def cas_table(length):
    index = np.arange(length)
    phase = (index[:, None] * index[None, :] % length) * (2.0 * np.pi / length)
    return (np.cos(phase) + np.sin(phase)) / math.sqrt(length)


def halves(table):
    table = np.asarray(table, np.float32)
    high = table.astype(bf16)
    low = (table - high.astype(np.float32)).astype(bf16)
    return np.stack([high, low])


def symbol_row(length):
    return 4.0 * np.sin(np.pi * np.arange(length) / length) ** 2


def tables():
    cas_x, cas_y, cas_z = cas_table(NX), cas_table(NY), cas_table(NZ)
    row = np.arange(NX)
    gathered = 8 * (row % 16) + row // 16
    row = np.arange(10 * 16)
    spread = (8 * (row % 16) + row // 16 - 1) % NX
    x_in, x_spread, y = halves(cas_x[:, gathered]), halves(cas_x[spread, :]), halves(cas_y)
    y_rows = [y[part, :, half * 128 : half * 128 + 128] for part in range(2) for half in range(2)]
    return {
        "spectral": np.concatenate([x_in[0], x_in[1], x_spread[0], x_spread[1], *y_rows]),
        "x": halves(cas_x),
        "y": y,
        "z": halves(cas_z),
        "symbol": np.asarray(symbol_row(NX)[:, None] + symbol_row(NY)[None, :], np.float32),
    }


def shift_of(frequency):
    phase = 2.0 * math.pi * frequency / STEPS
    return (1.0 - ROOT * math.cos(phase), ROOT * math.sin(phase) if frequency % 4 else 0.0)


def split(value):
    high = value.astype(bf16)
    return high, (value - high.astype(f32)).astype(bf16)


def dot(left, right):
    return jnp.dot(left, right, preferred_element_type=f32)


def left_mul(table, value):
    high, low = split(value)
    return dot(jnp.concatenate([table[0], table[1], table[0]], axis=1), jnp.concatenate([high, high, low], axis=0))


def right_mul(value, table):
    high, low = split(value)
    return dot(jnp.concatenate([high, high, low], axis=1), jnp.concatenate([table[0], table[1], table[0]], axis=0))


def spectral_parts(table_ref):
    x_in = table_ref[0:128, :], table_ref[128:256, :]
    x_spread = table_ref[256:416, :], table_ref[416:576, :]
    y = [
        jnp.concatenate([table_ref[row : row + 256, :], table_ref[row + 256 : row + 512, :]], axis=1)
        for row in (576, 1088)
    ]
    return x_in, x_spread, y


def vmem():
    return pl.BlockSpec(memory_space=pltpu.VMEM)


def smem():
    return pl.BlockSpec(memory_space=pltpu.SMEM)


def hbm():
    return pl.BlockSpec(memory_space=pltpu.HBM)


def shape(*dims):
    return jax.ShapeDtypeStruct(dims, f32)


def enter_kernel(
    place_ref,
    source_hbm,
    initial_hbm,
    kappa_hbm,
    z_hbm,
    out_ref,
    source_ref,
    initial_ref,
    kappa_ref,
    rim_ref,
    z_ref,
    sems,
):
    position = place_ref[0]
    first = jnp.where(position == 0, jnp.float32(1.0), jnp.float32(0.0))
    quarter = lax.rem(position, 4)
    half = pl.ds(pl.multiple_of(lax.rem(position, 2) * 128, 128), 128)
    table_copy = pltpu.make_async_copy(z_hbm, z_ref, sems.at[16])
    kappa_copy = pltpu.make_async_copy(kappa_hbm.at[pl.ds(2 * quarter, 2)], kappa_ref, sems.at[17])
    rim_copy = pltpu.make_async_copy(kappa_hbm.at[7 * (quarter // 2), half], rim_ref, sems.at[18])
    copies = [pltpu.make_async_copy(source_hbm.at[x], source_ref.at[x], sems.at[x]) for x in range(8)]
    added = [pltpu.make_async_copy(initial_hbm.at[x], initial_ref.at[x], sems.at[8 + x]) for x in range(8)]
    table_copy.start()
    for x in range(8):
        copies[x].start()
        added[x].start()
    kappa_copy.start()
    rim_copy.start()
    table_copy.wait()
    nt = (((1,), (1,)), ((), ()))
    dims = functools.partial(lax.dot_general, dimension_numbers=nt, preferred_element_type=f32)
    z_wide = jnp.concatenate([z_ref[0], z_ref[1], z_ref[0]], axis=1)
    for x in range(8):
        copies[x].wait()
        added[x].wait()
        high, low = split(source_ref[x] + first * initial_ref[x])
        freq = dims(z_wide, jnp.concatenate([high, high, low], axis=1))
        for yh in range(2):
            for block in range(16):
                out_ref[pl.ds(block * 8 * 17 + yh * 8 + x, 8, stride=17), :] = freq[
                    block * 8 : block * 8 + 8, yh * 128 : yh * 128 + 128
                ]
    kappa_copy.wait()
    rim_copy.wait()
    total = jnp.sum(kappa_ref[...].reshape(64, 8, 128), axis=0)
    whole = jnp.broadcast_to(jnp.sum(total, keepdims=True), (8, 128))
    rim = rim_ref[...].T
    for block in range(16):
        out_ref[pl.ds(block * 8 * 17 + 16, 8, stride=17), :] = jnp.where(
            position < 4, rim[block * 8 : block * 8 + 8], whole
        )


def precondition_fields(work, kappa, symbol_z, symbol_ref, out):
    symbol = symbol_ref[...] + symbol_z
    scaled = step_length * kappa * symbol
    for pair in range(4):
        first = work[pl.ds(pair * 256, 128), :]
        second = work[pl.ds(pair * 256 + 128, 128), :]
        if pair == 0:
            out[pl.ds(0, 128), :] = first / (shift_of(0)[0] + scaled)
            out[pl.ds(128, 128), :] = second / (shift_of(4)[0] + scaled)
        else:
            shift = shift_of(pair)
            denom = shift[0] + scaled
            inverse = 1.0 / (denom * denom + shift[1] * shift[1])
            real, imag = denom * inverse, shift[1] * inverse
            out[pl.ds(pair * 256, 128), :] = first * real + second * imag
            out[pl.ds(pair * 256 + 128, 128), :] = second * real - first * imag


def spectral_core(
    kappa, symbol_z, gathered, table_ref, symbol_ref, hat_ref, out_ref, work, count
):
    x_in_ref, x_spread_ref, y_ref = spectral_parts(table_ref)
    for field in range(8):
        work[pl.ds(field * 128, 128), :] = left_mul(x_in_ref, gathered[pl.ds(field * 128, 128), :])
    work[...] = right_mul(work[...], y_ref)
    precondition_fields(work, kappa, symbol_z, symbol_ref, hat_ref)
    work[...] = right_mul(hat_ref[...], y_ref)
    lane = lax.broadcasted_iota(jnp.int32, (8, 128), 1)
    for pair in range(4):
        edges = {}
        for part in range(2):
            spread = left_mul(x_spread_ref, work[pl.ds((pair * 2 + part) * 128, 128), :])
            for core in range(2):
                for block in range(2):
                    base = ((2 * pair + core) * 16 + block * 8) * count
                    edge = edges.get((core, block), jnp.zeros((8, 128), f32))
                    for x in range(10):
                        rows = spread[x * 16 + block * 8 : x * 16 + block * 8 + 8]
                        out_ref[pl.ds(base + part * 10 + x, 8, stride=count), :] = rows[:, core * 128 : core * 128 + 128]
                        if 1 <= x <= 8:
                            spot = 2 * (part * 8 + x - 1)
                            other = rows[:, (1 - core) * 128 : (1 - core) * 128 + 128]
                            edge = jnp.where(lane // 2 == spot // 2, pltpu.roll(other, spot + 1, 1), edge)
                    edges[core, block] = edge
        for core in range(2):
            for block in range(2):
                base = ((2 * pair + core) * 16 + block * 8) * count
                out_ref[pl.ds(base + 20, 8, stride=count), :] = edges[core, block]


def spectral_first_kernel(
    symbol_z_ref,
    in_ref,
    table_ref,
    symbol_ref,
    hat_ref,
    out_ref,
    kappa_ref,
    gathered,
    work,
):

    def extra(step, block):
        return in_ref[pl.ds((step * 16 + block * 8) * 17 + 16, 8, stride=17), :]

    row = lax.broadcasted_iota(jnp.int32, (8, 128), 0)
    for core in range(2):
        first, last = [extra(core, 0), extra(core, 1)], [extra(2 + core, 0), extra(2 + core, 1)]
        for block in range(2):
            low = jnp.where(row == 0, pltpu.roll(last[1 - block], 1, 0), pltpu.roll(last[block], 1, 0))
            high = jnp.where(row == 7, pltpu.roll(first[1 - block], 7, 0), pltpu.roll(first[block], 7, 0))
            for pair in range(4):
                base = ((2 * pair + core) * 16 + block * 8) * ROWS_FIRST
                out_ref[pl.ds(base + 21, 8, stride=ROWS_FIRST), :] = low
                out_ref[pl.ds(base + 22, 8, stride=ROWS_FIRST), :] = high
    parts = extra(4, 0) + extra(4, 1)
    for step in range(5, 8):
        parts = parts + (extra(step, 0) + extra(step, 1))
    kappa = jnp.sum(parts, axis=0, keepdims=True) * (1.0 / (NX * NY * NZ))
    kappa_ref[...] = jnp.broadcast_to(kappa, (8, 128))
    kappa = kappa[:, 0:1]
    for x in range(8):
        for block in range(2):
            for yh in range(2):
                lifted = []
                for step in range(8):
                    row = (step * 16 + block * 8) * 17 + yh * 8 + x
                    lifted.append(in_ref[pl.ds(row, 8, stride=17), :] * (alpha_corner ** (step / STEPS)))
                plus = [lifted[m] + lifted[m + 4] for m in range(4)]
                minus = [lifted[m] - lifted[m + 4] for m in range(4)]
                odd_minus = HALF * (minus[1] - minus[3])
                odd_plus = HALF * (minus[1] + minus[3])
                even, odd = plus[0] + plus[2], plus[1] + plus[3]
                fields = [
                    even + odd,
                    even - odd,
                    minus[0] + odd_minus,
                    -minus[2] - odd_plus,
                    plus[0] - plus[2],
                    plus[3] - plus[1],
                    minus[0] - odd_minus,
                    minus[2] - odd_plus,
                ]
                for field in range(8):
                    gathered[pl.ds(field * 128 + x * 16 + block * 8, 8), pl.ds(yh * 128, 128)] = fields[field]
    spectral_core(
        kappa, symbol_z_ref[0], gathered, table_ref, symbol_ref, hat_ref, out_ref, work, ROWS_FIRST
    )


def spectral_second_kernel(
    symbol_z_ref, kappa_ref, in_ref, table_ref, symbol_ref, hat_ref, out_ref, gathered, work
):
    for field in range(8):
        pair, part = field // 2, field % 2
        for core in range(2):
            for x in range(8):
                for block in range(2):
                    row = ((2 * pair + core) * 16 + block * 8) * 16 + part * 8 + x
                    gathered[pl.ds(field * 128 + x * 16 + block * 8, 8), pl.ds(core * 128, 128)] = in_ref[
                        pl.ds(row, 8, stride=16), :
                    ]
    kappa = kappa_ref[0:1, 0:1]
    spectral_core(
        kappa, symbol_z_ref[0], gathered, table_ref, symbol_ref, hat_ref, out_ref, work, ROWS
    )


def coefficients(sums):
    lane = lax.broadcasted_iota(jnp.int32, (4, 128), 1)

    def pick(number):
        return jnp.sum(jnp.where(lane == number, sums, 0.0), axis=1, keepdims=True)

    values = [pick(number) for number in range(16)]
    packed = lax.broadcasted_iota(jnp.int32, (4, 1), 0) == 0

    def complex_of(base):
        return values[base] + values[base + 1], values[base + 2] - values[base + 3]

    def solve(g11, g22, g12, h1, h2):
        scale1 = jnp.where(g11 > 0.0, lax.rsqrt(jnp.maximum(g11, 1e-37)), 0.0)
        scale2 = jnp.where(g22 > 0.0, lax.rsqrt(jnp.maximum(g22, 1e-37)), 0.0)
        corr = (g12[0] * scale1 * scale2, g12[1] * scale1 * scale2)
        t1 = (h1[0] * scale1, h1[1] * scale1)
        t2 = (h2[0] * scale2, h2[1] * scale2)
        det = 1.0 - (corr[0] * corr[0] + corr[1] * corr[1])
        good = jnp.logical_and(det > 1e-6, g22 > 0.0)
        inv = jnp.where(good, 1.0 / jnp.where(good, det, 1.0), 0.0)
        one = (
            jnp.where(good, (t1[0] - (corr[0] * t2[0] - corr[1] * t2[1])) * inv, t1[0]),
            jnp.where(good, (t1[1] - (corr[0] * t2[1] + corr[1] * t2[0])) * inv, t1[1]),
        )
        two = (
            (t2[0] - (corr[0] * t1[0] + corr[1] * t1[1])) * inv,
            (t2[1] - (corr[0] * t1[1] - corr[1] * t1[0])) * inv,
        )
        return (1.0 - one[0] * scale1, -one[1] * scale1), (-two[0] * scale2, -two[1] * scale2)

    zero = jnp.zeros((4, 1), f32)
    full = solve(values[0] + values[1], values[2] + values[3], complex_of(4), complex_of(8), complex_of(12))
    first = solve(values[0], values[2], (values[4], zero), (values[8], zero), (values[12], zero))
    second = solve(values[1], values[3], (values[5], zero), (values[9], zero), (values[13], zero))
    maps = []
    for vector in range(2):
        maps.append(
            (
                jnp.where(packed, first[vector][0], full[vector][0]),
                jnp.where(packed, 0.0, full[vector][1]),
                jnp.where(packed, second[vector][0], full[vector][0]),
            )
        )
    return maps


def spectral_last_kernel(sums_ref, hat_one_ref, hat_two_ref, x_ref, y_ref, out_ref, work):
    sums = jnp.concatenate(
        [jnp.sum(sums_ref[pl.ds(pair * 32, 32), :], axis=0, keepdims=True) for pair in range(4)], axis=0
    )
    maps = coefficients(sums)
    scales = [[[entry[pair : pair + 1, :] for entry in vector] for pair in range(4)] for vector in maps]
    for block in range(16):
        rows = 8
        fields = []
        for pair in range(4):
            parts = []
            for hat in (hat_one_ref, hat_two_ref):
                parts.append(
                    (
                        hat[pl.ds(pair * 256 + block * rows, rows), :],
                        hat[pl.ds(pair * 256 + 128 + block * rows, rows), :],
                    )
                )
            (p1, q1), (p2, q2) = parts
            (a1, b1, c1), (a2, b2, c2) = scales[0][pair], scales[1][pair]
            fields.append(a1 * p1 - b1 * q1 + (a2 * p2 - b2 * q2))
            fields.append(c1 * q1 + b1 * p1 + (c2 * q2 + b2 * p2))
        zero, four, re1, im1, re2, im2, re3, im3 = fields
        even = [zero + four + 2.0 * re2, zero - four - 2.0 * im2, zero + four - 2.0 * re2, zero - four + 2.0 * im2]
        diff, total = (2.0 * HALF) * (re1 - re3), (2.0 * HALF) * (im1 + im3)
        odd = [2.0 * (re1 + re3), diff - total, 2.0 * (im3 - im1), -diff - total]
        for step in range(8):
            value = even[step % 4] + odd[step % 4] if step < 4 else even[step % 4] - odd[step % 4]
            scale = alpha_corner ** (-step / STEPS) / STEPS
            work[pl.ds(step * 128 + block * rows, rows), :] = value * scale
    work[...] = right_mul(work[...], y_ref)
    for step in range(8):
        planes = left_mul(x_ref, work[pl.ds(step * 128, 128), :])
        for slab in range(16):
            for yh in range(2):
                out_ref[pl.ds((step * 16 + slab) * 16 + yh * 8, 8), :] = planes[
                    slab * 8 : slab * 8 + 8, yh * 128 : yh * 128 + 128
                ]


def faces_kernel(place_ref, kappa_ref, faces_ref):
    upper = lax.rem(place_ref[0], 2) == 1

    def half(plane):
        return jnp.where(upper, plane[128:], plane[:128]).T

    before = None
    for x in range(8):
        whole = kappa_ref[x]
        here = half(whole)
        faces_ref[9 + x] = 0.5 * (here + half(pltpu.roll(whole, NY - 1, 0)))
        faces_ref[17 + x] = 0.5 * (here + half(pltpu.roll(whole, 1, 0)))
        faces_ref[25 + x] = 0.5 * (here + pltpu.roll(here, NZ - 1, 0))
        faces_ref[33 + x] = 0.5 * (here + pltpu.roll(here, 1, 0))
        if x == 0:
            faces_ref[0] = here
        else:
            faces_ref[x] = 0.5 * (before + here)
        before = here
    faces_ref[8] = before


def column(in_ref, number, count):
    return jnp.concatenate(
        [in_ref[pl.ds(block * 8 * count + number, 8, stride=count), :] for block in range(16)], axis=0
    )


def load_block(in_ref, z_ref, field, count):
    for number in range(0, 20, 2):
        columns = [column(in_ref, number + step, count) for step in range(2)]
        both = left_mul(z_ref, jnp.concatenate(columns, axis=1))
        field[number] = both[:, :128]
        field[number + 1] = both[:, 128:]
    field[20] = left_mul(z_ref, column(in_ref, 20, count))


def beside(field, part, x, lane):
    here = field[part * 10 + x + 1]
    spot = 2 * (part * 8 + x)
    edge = field[20]
    below = jnp.where(lane == 0, pltpu.roll(edge, (128 - spot) % 128, 1), pltpu.roll(here, 1, 1))
    above = jnp.where(lane == 127, pltpu.roll(edge, 126 - spot, 1), pltpu.roll(here, 127, 1))
    return here, below, above


def slopes(field, part, x, lane):
    here, below, above = beside(field, part, x, lane)
    others = [field[part * 10 + x], field[part * 10 + x + 2], above, below]
    others += [pltpu.roll(here, NZ - 1, 0), pltpu.roll(here, 1, 0)]
    return here, [here - other for other in others]


def weights(faces_ref, ends_ref, x, kappa):
    low = ends_ref[0] if x == 0 else faces_ref[x]
    high = ends_ref[1] if x == 7 else faces_ref[x + 1]
    terms = [low, high] + [faces_ref[8 * number + 1 + x] for number in range(1, 5)]
    return [term - kappa for term in terms]


def weighted(terms, values):
    total = [term * value for term, value in zip(terms, values)]
    return ((total[0] + total[1]) + (total[2] + total[3])) + (total[4] + total[5])


def block_first_kernel(
    place_ref, kappa_ref, in_ref, z_ref, faces_ref, out_ref, differ_ref, right_ref, ends_ref, field
):
    kappa = kappa_ref[0:1, 0:1]
    pair = place_ref[0] // 2
    real = [jnp.float32(shift_of(4 * part)[0]) for part in range(2)]
    imag = jnp.float32(0.0)
    for number in range(1, 4):
        real = [jnp.where(pair == number, shift_of(number)[0], value) for value in real]
        imag = jnp.where(pair == number, shift_of(number)[1], imag)
    load_block(in_ref, z_ref, field, ROWS_FIRST)
    ends_ref[0] = 0.5 * (column(in_ref, 21, ROWS_FIRST) + faces_ref[0])
    ends_ref[1] = 0.5 * (column(in_ref, 22, ROWS_FIRST) + faces_ref[8])
    lane = lax.broadcasted_iota(jnp.int32, (NZ, 128), 1)
    for x in range(8):
        values = []
        terms = weights(faces_ref, ends_ref, x, kappa)
        for part in range(2):
            here, slope = slopes(field, part, x, lane)
            value = weighted(terms, slope)
            differ_ref[part, x] = value
            values.append(value)
            other = field[(1 - part) * 10 + x + 1]
            cross = -imag if part == 0 else imag
            right_ref[part, x] = (
                real[part] * here
                + cross * other
                + (step_length * kappa) * (((slope[0] + slope[1]) + (slope[2] + slope[3])) + (slope[4] + slope[5]))
            )
        freq = left_mul(z_ref, jnp.concatenate(values, axis=1))
        for part in range(2):
            for block in range(16):
                out_ref[pl.ds(block * 8 * 16 + part * 8 + x, 8, stride=16), :] = freq[
                    block * 8 : block * 8 + 8, part * 128 : part * 128 + 128
                ]


def block_second_kernel(
    kappa_ref, in_ref, differ_ref, right_ref, z_ref, faces_ref, ends_ref, out_ref, field
):
    kappa = kappa_ref[0:1, 0:1]
    load_block(in_ref, z_ref, field, ROWS)
    lane = lax.broadcasted_iota(jnp.int32, (NZ, 128), 1)
    totals = [jnp.zeros((8, 128), f32) for _ in range(16)]

    def fold(value):
        return jnp.sum(value.reshape(16, 8, 128), axis=0)

    for x in range(8):
        diffs = [differ_ref[part, x] for part in range(2)]
        ones = [right_ref[part, x] + diffs[part] for part in range(2)]
        terms = weights(faces_ref, ends_ref, x, kappa)
        twos = [diffs[part] + weighted(terms, slopes(field, part, x, lane)[1]) for part in range(2)]
        pairs = [(ones[0], ones[0]), (ones[1], ones[1]), (twos[0], twos[0]), (twos[1], twos[1])]
        for left, right in ((ones, twos), (ones, diffs), (twos, diffs)):
            pairs += [(left[0], right[0]), (left[1], right[1]), (left[0], right[1]), (left[1], right[0])]
        for number, (left, right) in enumerate(pairs):
            totals[number] = totals[number] + fold(left * right)
    spot = lax.broadcasted_iota(jnp.int32, (1, 128), 1)
    row = jnp.zeros((1, 128), f32)
    for number in range(16):
        row = row + jnp.where(spot == number, jnp.sum(totals[number], keepdims=True), 0.0)
    out_ref[...] = jnp.broadcast_to(row, (DEVS, 128))


def leave_kernel(in_ref, z_ref, out_hbm, out_ref, sems):
    copies = [pltpu.make_async_copy(out_ref.at[x], out_hbm.at[0, x], sems.at[x]) for x in range(8)]
    for x in range(8):
        columns = []
        for yh in range(2):
            rows = [in_ref[pl.ds(block * 8 * 16 + yh * 8 + x, 8, stride=16), :] for block in range(16)]
            columns.append(jnp.concatenate(rows, axis=0))
        value = left_mul(z_ref, jnp.concatenate(columns, axis=1))
        out_ref[x] = value.T
        copies[x].start()
    for copy in copies:
        copy.wait()


def exchange(rows):
    wide = rows.reshape(rows.shape[0], 1, 128)
    return lax.all_to_all(wide, BOTH, split_axis=0, concat_axis=0, tiled=True).reshape(rows.shape)


def call(kernel, outs, scalars, scratch, *args, far_in=(), far_out=()):
    args = [
        pltpu.with_memory_space_constraint(arg, pltpu.HBM) if number in far_in else arg
        for number, arg in enumerate(args)
    ]
    outs = [pltpu.HBM(out.shape, out.dtype) if number in far_out else out for number, out in enumerate(outs)]
    return pl.pallas_call(
        kernel,
        out_shape=outs,
        in_specs=[
            smem() if number < scalars else (hbm() if number in far_in else vmem()) for number in range(len(args))
        ],
        out_specs=[hbm() if number in far_out else vmem() for number in range(len(outs))],
        scratch_shapes=scratch,
        name=kernel.__name__,
        compiler_params=pltpu.CompilerParams(vmem_limit_bytes=16 << 20),
    )(*args)


def shards(source, initial, diffusivity):
    table = tables()
    position = lax.axis_index("tm")
    slab = lax.axis_index("space")
    wave = (position * SLABS + slab).astype(f32)
    symbol_z = (4.0 * jnp.sin(math.pi * wave / NZ) ** 2).reshape(1)
    place = position.astype(jnp.int32).reshape(1)
    source, place, symbol_z = lax.optimization_barrier((source, place, symbol_z))

    slab_block = pltpu.VMEM((8, NY, NZ), f32)
    (rows,) = call(
        enter_kernel,
        [shape(DEVS * 17, 128)],
        1,
        [
            slab_block,
            slab_block,
            pltpu.VMEM((2, NY, NZ), f32),
            pltpu.VMEM((128, NZ), f32),
            pltpu.VMEM((2, NZ, NZ), bf16),
            pltpu.SemaphoreType.DMA((19,)),
        ],
        place,
        source[0],
        initial,
        diffusivity,
        table["z"],
        far_in=(1, 2, 3, 4),
    )
    rows = exchange(rows)
    big = pltpu.VMEM((1024, NY), f32)
    hat_one, rows, kappa = call(
        spectral_first_kernel,
        [shape(1024, NY), shape(DEVS * ROWS_FIRST, 128), shape(8, 128)],
        1,
        [big, big],
        symbol_z,
        rows,
        table["spectral"],
        table["symbol"],
    )
    rows, diffusivity = lax.optimization_barrier((rows, diffusivity))
    (faces,) = call(faces_kernel, [shape(41, NZ, 128)], 1, [], place, diffusivity)
    rows, faces = lax.optimization_barrier((rows, faces))
    rows = exchange(rows)
    block = pltpu.VMEM((21, NZ, 128), f32)
    rows, differ, right, ends = call(
        block_first_kernel,
        [shape(DEVS * 16, 128), shape(2, 8, NZ, 128), shape(2, 8, NZ, 128), shape(2, NZ, 128)],
        1,
        [block],
        place,
        kappa,
        rows,
        table["z"],
        faces,
    )
    rows = exchange(rows)
    hat_two, rows = call(
        spectral_second_kernel,
        [shape(1024, NY), shape(DEVS * ROWS, 128)],
        1,
        [big, big],
        symbol_z,
        kappa,
        rows,
        table["spectral"],
        table["symbol"],
    )
    rows = exchange(rows)
    (sums,) = call(block_second_kernel, [shape(DEVS, 128)], 0, [block], kappa, rows, differ, right, table["z"], faces, ends)
    sums = exchange(sums)
    (rows,) = call(
        spectral_last_kernel, [shape(DEVS * 16, 128)], 0, [big], sums, hat_one, hat_two, table["x"], table["y"]
    )
    rows = exchange(rows)
    (field,) = call(
        leave_kernel,
        [shape(1, 8, NY, NZ)],
        0,
        [slab_block, pltpu.SemaphoreType.DMA((8,))],
        rows,
        table["z"],
        far_out=(0,),
    )
    return field


def solution(mesh):
    in_specs = (P("tm", "space", None, None), P("space", None, None), P("space", None, None))
    out_specs = P("tm", "space", None, None)
    return jax.shard_map(shards, mesh=mesh, in_specs=in_specs, out_specs=out_specs, check_vma=False)
```

```python
import functools
import math

import jax
import jax.numpy as jnp
import numpy as np
from jax import lax
from jax.experimental import pallas as pl
from jax.experimental.pallas import tpu as pltpu
from jax.sharding import PartitionSpec as P


alpha_corner = 0.05
step_length = 1.0
BOTH = ("tm", "space")
NX, NY, NZ = 128, 256, 128
STEPS = 8
ROWS = 21
ROWS_FIRST = 23
SLABS = 16
DEVS = 128
GROUPS = ((0, 1), (1, 3), (3, 8))
f32 = jnp.float32
bf16 = jnp.bfloat16
ROOT = alpha_corner ** (1.0 / STEPS)
HALF = math.sqrt(0.5)


def cas_table(length):
    index = np.arange(length)
    phase = (index[:, None] * index[None, :] % length) * (2.0 * np.pi / length)
    return (np.cos(phase) + np.sin(phase)) / math.sqrt(length)


def halves(table):
    table = np.asarray(table, np.float32)
    high = table.astype(bf16)
    low = (table - high.astype(np.float32)).astype(bf16)
    return np.stack([high, low])


def symbol_row(length):
    return 4.0 * np.sin(np.pi * np.arange(length) / length) ** 2


def tables():
    cas_x, cas_y, cas_z = cas_table(NX), cas_table(NY), cas_table(NZ)
    row = np.arange(NX)
    gathered = 8 * (row % 16) + row // 16
    row = np.arange(10 * 16)
    spread = (8 * (row % 16) + row // 16 - 1) % NX
    x_in, x_spread, y = halves(cas_x[:, gathered]), halves(cas_x[spread, :]), halves(cas_y)
    y_rows = [y[part, :, half * 128 : half * 128 + 128] for part in range(2) for half in range(2)]
    return {
        "spectral": np.concatenate([x_in[0], x_in[1], x_spread[0], x_spread[1], *y_rows]),
        "x": halves(cas_x),
        "y": y,
        "z": halves(cas_z),
        "symbol": np.asarray(symbol_row(NX)[:, None] + symbol_row(NY)[None, :], np.float32),
    }


def shift_of(frequency):
    phase = 2.0 * math.pi * frequency / STEPS
    return (1.0 - ROOT * math.cos(phase), ROOT * math.sin(phase) if frequency % 4 else 0.0)


def split(value):
    high = value.astype(bf16)
    return high, (value - high.astype(f32)).astype(bf16)


def dot(left, right):
    return jnp.dot(left, right, preferred_element_type=f32)


def left_mul(table, value):
    high, low = split(value)
    return dot(jnp.concatenate([table[0], table[1], table[0]], axis=1), jnp.concatenate([high, high, low], axis=0))


def right_mul(value, table):
    high, low = split(value)
    return dot(jnp.concatenate([high, high, low], axis=1), jnp.concatenate([table[0], table[1], table[0]], axis=0))


def spectral_parts(table_ref):
    x_in = table_ref[0:128, :], table_ref[128:256, :]
    x_spread = table_ref[256:416, :], table_ref[416:576, :]
    y = [
        jnp.concatenate([table_ref[row : row + 256, :], table_ref[row + 256 : row + 512, :]], axis=1)
        for row in (576, 1088)
    ]
    return x_in, x_spread, y


def vmem():
    return pl.BlockSpec(memory_space=pltpu.VMEM)


def smem():
    return pl.BlockSpec(memory_space=pltpu.SMEM)


def hbm():
    return pl.BlockSpec(memory_space=pltpu.HBM)


def shape(*dims):
    return jax.ShapeDtypeStruct(dims, f32)


def enter_kernel(
    place_ref,
    source_hbm,
    initial_hbm,
    kappa_hbm,
    z_hbm,
    out_ref,
    source_ref,
    initial_ref,
    kappa_ref,
    rim_ref,
    z_ref,
    sems,
):
    position = place_ref[0]
    first = jnp.where(position == 0, jnp.float32(1.0), jnp.float32(0.0))
    quarter = lax.rem(position, 4)
    half = pl.ds(pl.multiple_of(lax.rem(position, 2) * 128, 128), 128)
    table_copy = pltpu.make_async_copy(z_hbm, z_ref, sems.at[16])
    kappa_copy = pltpu.make_async_copy(kappa_hbm.at[pl.ds(2 * quarter, 2)], kappa_ref, sems.at[17])
    rim_copy = pltpu.make_async_copy(kappa_hbm.at[7 * (quarter // 2), half], rim_ref, sems.at[18])
    copies, added = [], []
    for number, (begin, end) in enumerate(GROUPS):
        planes = pl.ds(begin, end - begin)
        copies.append(pltpu.make_async_copy(source_hbm.at[planes], source_ref.at[planes], sems.at[number]))
        added.append(pltpu.make_async_copy(initial_hbm.at[planes], initial_ref.at[planes], sems.at[8 + number]))
    copies[0].start()
    added[0].start()
    table_copy.start()
    for copy, other in zip(copies[1:], added[1:]):
        copy.start()
        other.start()
    kappa_copy.start()
    rim_copy.start()
    table_copy.wait()
    nt = (((1,), (1,)), ((), ()))
    dims = functools.partial(lax.dot_general, dimension_numbers=nt, preferred_element_type=f32)
    z_wide = jnp.concatenate([z_ref[0], z_ref[1], z_ref[0]], axis=1)
    starts = {begin: number for number, (begin, _) in enumerate(GROUPS)}
    for x in range(8):
        if x in starts:
            copies[starts[x]].wait()
            added[starts[x]].wait()
        high, low = split(source_ref[x] + first * initial_ref[x])
        freq = dims(z_wide, jnp.concatenate([high, high, low], axis=1))
        for yh in range(2):
            for block in range(16):
                out_ref[pl.ds(block * 8 * 17 + yh * 8 + x, 8, stride=17), :] = freq[
                    block * 8 : block * 8 + 8, yh * 128 : yh * 128 + 128
                ]
    kappa_copy.wait()
    rim_copy.wait()
    total = jnp.sum(kappa_ref[...].reshape(64, 8, 128), axis=0)
    whole = jnp.broadcast_to(jnp.sum(total, keepdims=True), (8, 128))
    rim = rim_ref[...].T
    for block in range(16):
        out_ref[pl.ds(block * 8 * 17 + 16, 8, stride=17), :] = jnp.where(
            position < 4, rim[block * 8 : block * 8 + 8], whole
        )


def precondition_fields(work, kappa, symbol_z, symbol_ref, out):
    symbol = symbol_ref[...] + symbol_z
    scaled = step_length * kappa * symbol
    for pair in range(4):
        first = work[pl.ds(pair * 256, 128), :]
        second = work[pl.ds(pair * 256 + 128, 128), :]
        if pair == 0:
            out[pl.ds(0, 128), :] = first / (shift_of(0)[0] + scaled)
            out[pl.ds(128, 128), :] = second / (shift_of(4)[0] + scaled)
        else:
            shift = shift_of(pair)
            denom = shift[0] + scaled
            inverse = 1.0 / (denom * denom + shift[1] * shift[1])
            real, imag = denom * inverse, shift[1] * inverse
            out[pl.ds(pair * 256, 128), :] = first * real + second * imag
            out[pl.ds(pair * 256 + 128, 128), :] = second * real - first * imag


def spectral_core(
    kappa, symbol_z, gathered, table_ref, symbol_ref, hat_ref, out_ref, work, count
):
    x_in_ref, x_spread_ref, y_ref = spectral_parts(table_ref)
    for field in range(8):
        work[pl.ds(field * 128, 128), :] = left_mul(x_in_ref, gathered[pl.ds(field * 128, 128), :])
    work[...] = right_mul(work[...], y_ref)
    precondition_fields(work, kappa, symbol_z, symbol_ref, hat_ref)
    work[...] = right_mul(hat_ref[...], y_ref)
    lane = lax.broadcasted_iota(jnp.int32, (8, 128), 1)
    for pair in range(4):
        edges = {}
        for part in range(2):
            spread = left_mul(x_spread_ref, work[pl.ds((pair * 2 + part) * 128, 128), :])
            for core in range(2):
                for block in range(2):
                    base = ((2 * pair + core) * 16 + block * 8) * count
                    edge = edges.get((core, block), jnp.zeros((8, 128), f32))
                    for x in range(10):
                        rows = spread[x * 16 + block * 8 : x * 16 + block * 8 + 8]
                        out_ref[pl.ds(base + part * 10 + x, 8, stride=count), :] = rows[:, core * 128 : core * 128 + 128]
                        if 1 <= x <= 8:
                            spot = 2 * (part * 8 + x - 1)
                            other = rows[:, (1 - core) * 128 : (1 - core) * 128 + 128]
                            edge = jnp.where(lane // 2 == spot // 2, pltpu.roll(other, spot + 1, 1), edge)
                    edges[core, block] = edge
        for core in range(2):
            for block in range(2):
                base = ((2 * pair + core) * 16 + block * 8) * count
                out_ref[pl.ds(base + 20, 8, stride=count), :] = edges[core, block]


def spectral_first_kernel(
    symbol_z_ref,
    in_ref,
    table_ref,
    symbol_ref,
    hat_ref,
    out_ref,
    kappa_ref,
    gathered,
    work,
):

    def extra(step, block):
        return in_ref[pl.ds((step * 16 + block * 8) * 17 + 16, 8, stride=17), :]

    row = lax.broadcasted_iota(jnp.int32, (8, 128), 0)
    for core in range(2):
        first, last = [extra(core, 0), extra(core, 1)], [extra(2 + core, 0), extra(2 + core, 1)]
        for block in range(2):
            low = jnp.where(row == 0, pltpu.roll(last[1 - block], 1, 0), pltpu.roll(last[block], 1, 0))
            high = jnp.where(row == 7, pltpu.roll(first[1 - block], 7, 0), pltpu.roll(first[block], 7, 0))
            for pair in range(4):
                base = ((2 * pair + core) * 16 + block * 8) * ROWS_FIRST
                out_ref[pl.ds(base + 21, 8, stride=ROWS_FIRST), :] = low
                out_ref[pl.ds(base + 22, 8, stride=ROWS_FIRST), :] = high
    parts = extra(4, 0) + extra(4, 1)
    for step in range(5, 8):
        parts = parts + (extra(step, 0) + extra(step, 1))
    kappa = jnp.sum(parts, axis=0, keepdims=True) * (1.0 / (NX * NY * NZ))
    kappa_ref[...] = jnp.broadcast_to(kappa, (8, 128))
    kappa = kappa[:, 0:1]
    for x in range(8):
        for block in range(2):
            for yh in range(2):
                lifted = []
                for step in range(8):
                    row = (step * 16 + block * 8) * 17 + yh * 8 + x
                    lifted.append(in_ref[pl.ds(row, 8, stride=17), :] * (alpha_corner ** (step / STEPS)))
                plus = [lifted[m] + lifted[m + 4] for m in range(4)]
                minus = [lifted[m] - lifted[m + 4] for m in range(4)]
                odd_minus = HALF * (minus[1] - minus[3])
                odd_plus = HALF * (minus[1] + minus[3])
                even, odd = plus[0] + plus[2], plus[1] + plus[3]
                fields = [
                    even + odd,
                    even - odd,
                    minus[0] + odd_minus,
                    -minus[2] - odd_plus,
                    plus[0] - plus[2],
                    plus[3] - plus[1],
                    minus[0] - odd_minus,
                    minus[2] - odd_plus,
                ]
                for field in range(8):
                    gathered[pl.ds(field * 128 + x * 16 + block * 8, 8), pl.ds(yh * 128, 128)] = fields[field]
    spectral_core(
        kappa, symbol_z_ref[0], gathered, table_ref, symbol_ref, hat_ref, out_ref, work, ROWS_FIRST
    )


def spectral_second_kernel(
    symbol_z_ref, kappa_ref, in_ref, table_ref, symbol_ref, hat_ref, out_ref, gathered, work
):
    for field in range(8):
        pair, part = field // 2, field % 2
        for core in range(2):
            for x in range(8):
                for block in range(2):
                    row = ((2 * pair + core) * 16 + block * 8) * 16 + part * 8 + x
                    gathered[pl.ds(field * 128 + x * 16 + block * 8, 8), pl.ds(core * 128, 128)] = in_ref[
                        pl.ds(row, 8, stride=16), :
                    ]
    kappa = kappa_ref[0:1, 0:1]
    spectral_core(
        kappa, symbol_z_ref[0], gathered, table_ref, symbol_ref, hat_ref, out_ref, work, ROWS
    )


def coefficients(sums):
    lane = lax.broadcasted_iota(jnp.int32, (4, 128), 1)

    def pick(number):
        return jnp.sum(jnp.where(lane == number, sums, 0.0), axis=1, keepdims=True)

    values = [pick(number) for number in range(16)]
    packed = lax.broadcasted_iota(jnp.int32, (4, 1), 0) == 0

    def complex_of(base):
        return values[base] + values[base + 1], values[base + 2] - values[base + 3]

    def solve(g11, g22, g12, h1, h2):
        scale1 = jnp.where(g11 > 0.0, lax.rsqrt(jnp.maximum(g11, 1e-37)), 0.0)
        scale2 = jnp.where(g22 > 0.0, lax.rsqrt(jnp.maximum(g22, 1e-37)), 0.0)
        corr = (g12[0] * scale1 * scale2, g12[1] * scale1 * scale2)
        t1 = (h1[0] * scale1, h1[1] * scale1)
        t2 = (h2[0] * scale2, h2[1] * scale2)
        det = 1.0 - (corr[0] * corr[0] + corr[1] * corr[1])
        good = jnp.logical_and(det > 1e-6, g22 > 0.0)
        inv = jnp.where(good, 1.0 / jnp.where(good, det, 1.0), 0.0)
        one = (
            jnp.where(good, (t1[0] - (corr[0] * t2[0] - corr[1] * t2[1])) * inv, t1[0]),
            jnp.where(good, (t1[1] - (corr[0] * t2[1] + corr[1] * t2[0])) * inv, t1[1]),
        )
        two = (
            (t2[0] - (corr[0] * t1[0] + corr[1] * t1[1])) * inv,
            (t2[1] - (corr[0] * t1[1] - corr[1] * t1[0])) * inv,
        )
        return (1.0 - one[0] * scale1, -one[1] * scale1), (-two[0] * scale2, -two[1] * scale2)

    zero = jnp.zeros((4, 1), f32)
    full = solve(values[0] + values[1], values[2] + values[3], complex_of(4), complex_of(8), complex_of(12))
    first = solve(values[0], values[2], (values[4], zero), (values[8], zero), (values[12], zero))
    second = solve(values[1], values[3], (values[5], zero), (values[9], zero), (values[13], zero))
    maps = []
    for vector in range(2):
        maps.append(
            (
                jnp.where(packed, first[vector][0], full[vector][0]),
                jnp.where(packed, 0.0, full[vector][1]),
                jnp.where(packed, second[vector][0], full[vector][0]),
            )
        )
    return maps


def unfold_kernel(hat_one_ref, hat_two_ref, x_ref, y_ref, one_ref, two_ref, work):
    for hat, out in ((hat_one_ref, one_ref), (hat_two_ref, two_ref)):
        work[...] = right_mul(hat[...], y_ref)
        for field in range(8):
            rows = pl.ds(field * 128, 128)
            out[rows, :] = left_mul(x_ref, work[rows, :])


def combine_kernel(sums_ref, one_ref, two_ref, out_ref):
    sums = jnp.concatenate(
        [jnp.sum(sums_ref[pl.ds(pair * 32, 32), :], axis=0, keepdims=True) for pair in range(4)], axis=0
    )
    maps = coefficients(sums)
    scales = [
        [[jnp.broadcast_to(entry[pair : pair + 1, :], (8, NY)) for entry in vector] for pair in range(4)]
        for vector in maps
    ]
    for slab in range(16):
        fields = []
        for pair in range(4):
            parts = []
            for ref in (one_ref, two_ref):
                row = pair * 256 + slab * 8
                parts.append((ref[pl.ds(row, 8), :], ref[pl.ds(row + 128, 8), :]))
            (p1, q1), (p2, q2) = parts
            (a1, b1, c1), (a2, b2, c2) = scales[0][pair], scales[1][pair]
            fields.append(a1 * p1 - b1 * q1 + (a2 * p2 - b2 * q2))
            fields.append(c1 * q1 + b1 * p1 + (c2 * q2 + b2 * p2))
        zero, four, re1, im1, re2, im2, re3, im3 = fields
        even = [zero + four + 2.0 * re2, zero - four - 2.0 * im2, zero + four - 2.0 * re2, zero - four + 2.0 * im2]
        diff, total = (2.0 * HALF) * (re1 - re3), (2.0 * HALF) * (im1 + im3)
        odd = [2.0 * (re1 + re3), diff - total, 2.0 * (im3 - im1), -diff - total]
        for step in range(8):
            value = even[step % 4] + odd[step % 4] if step < 4 else even[step % 4] - odd[step % 4]
            value = value * (alpha_corner ** (-step / STEPS) / STEPS)
            for yh in range(2):
                out_ref[pl.ds((step * 16 + slab) * 16 + yh * 8, 8), :] = value[:, yh * 128 : yh * 128 + 128]


def faces_kernel(place_ref, kappa_ref, faces_ref):
    upper = lax.rem(place_ref[0], 2) == 1

    def half(plane):
        return jnp.where(upper, plane[128:], plane[:128]).T

    before = None
    for x in range(8):
        whole = kappa_ref[x]
        here = half(whole)
        faces_ref[9 + x] = 0.5 * (here + half(pltpu.roll(whole, NY - 1, 0)))
        faces_ref[17 + x] = 0.5 * (here + half(pltpu.roll(whole, 1, 0)))
        faces_ref[25 + x] = 0.5 * (here + pltpu.roll(here, NZ - 1, 0))
        faces_ref[33 + x] = 0.5 * (here + pltpu.roll(here, 1, 0))
        if x == 0:
            faces_ref[0] = here
        else:
            faces_ref[x] = 0.5 * (before + here)
        before = here
    faces_ref[8] = before


def column(in_ref, number, count):
    return jnp.concatenate(
        [in_ref[pl.ds(block * 8 * count + number, 8, stride=count), :] for block in range(16)], axis=0
    )


def load_block(in_ref, z_ref, field, count):
    for number in range(0, 20, 2):
        columns = [column(in_ref, number + step, count) for step in range(2)]
        both = left_mul(z_ref, jnp.concatenate(columns, axis=1))
        field[number] = both[:, :128]
        field[number + 1] = both[:, 128:]
    field[20] = left_mul(z_ref, column(in_ref, 20, count))


def beside(field, part, x, lane):
    here = field[part * 10 + x + 1]
    spot = 2 * (part * 8 + x)
    edge = field[20]
    below = jnp.where(lane == 0, pltpu.roll(edge, (128 - spot) % 128, 1), pltpu.roll(here, 1, 1))
    above = jnp.where(lane == 127, pltpu.roll(edge, 126 - spot, 1), pltpu.roll(here, 127, 1))
    return here, below, above


def slopes(field, part, x, lane):
    here, below, above = beside(field, part, x, lane)
    others = [field[part * 10 + x], field[part * 10 + x + 2], above, below]
    others += [pltpu.roll(here, NZ - 1, 0), pltpu.roll(here, 1, 0)]
    return here, [here - other for other in others]


def weights(faces_ref, ends_ref, x, kappa):
    low = ends_ref[0] if x == 0 else faces_ref[x]
    high = ends_ref[1] if x == 7 else faces_ref[x + 1]
    terms = [low, high] + [faces_ref[8 * number + 1 + x] for number in range(1, 5)]
    return [term - kappa for term in terms]


def weighted(terms, values):
    total = [term * value for term, value in zip(terms, values)]
    return ((total[0] + total[1]) + (total[2] + total[3])) + (total[4] + total[5])


def block_first_kernel(
    place_ref, kappa_ref, in_ref, z_ref, faces_ref, out_ref, differ_ref, right_ref, ends_ref, field
):
    kappa = kappa_ref[0:1, 0:1]
    pair = place_ref[0] // 2
    real = [jnp.float32(shift_of(4 * part)[0]) for part in range(2)]
    imag = jnp.float32(0.0)
    for number in range(1, 4):
        real = [jnp.where(pair == number, shift_of(number)[0], value) for value in real]
        imag = jnp.where(pair == number, shift_of(number)[1], imag)
    load_block(in_ref, z_ref, field, ROWS_FIRST)
    ends_ref[0] = 0.5 * (column(in_ref, 21, ROWS_FIRST) + faces_ref[0])
    ends_ref[1] = 0.5 * (column(in_ref, 22, ROWS_FIRST) + faces_ref[8])
    lane = lax.broadcasted_iota(jnp.int32, (NZ, 128), 1)
    for x in range(8):
        values = []
        terms = weights(faces_ref, ends_ref, x, kappa)
        for part in range(2):
            here, slope = slopes(field, part, x, lane)
            value = weighted(terms, slope)
            differ_ref[part, x] = value
            values.append(value)
            other = field[(1 - part) * 10 + x + 1]
            cross = -imag if part == 0 else imag
            right_ref[part, x] = (
                real[part] * here
                + cross * other
                + (step_length * kappa) * (((slope[0] + slope[1]) + (slope[2] + slope[3])) + (slope[4] + slope[5]))
            )
        freq = left_mul(z_ref, jnp.concatenate(values, axis=1))
        for part in range(2):
            for block in range(16):
                out_ref[pl.ds(block * 8 * 16 + part * 8 + x, 8, stride=16), :] = freq[
                    block * 8 : block * 8 + 8, part * 128 : part * 128 + 128
                ]


def block_second_kernel(
    kappa_ref, in_ref, differ_ref, right_ref, z_ref, faces_ref, ends_ref, out_ref, field
):
    kappa = kappa_ref[0:1, 0:1]
    load_block(in_ref, z_ref, field, ROWS)
    lane = lax.broadcasted_iota(jnp.int32, (NZ, 128), 1)
    totals = [jnp.zeros((8, 128), f32) for _ in range(16)]

    def fold(value):
        return jnp.sum(value.reshape(16, 8, 128), axis=0)

    for x in range(8):
        diffs = [differ_ref[part, x] for part in range(2)]
        ones = [right_ref[part, x] + diffs[part] for part in range(2)]
        terms = weights(faces_ref, ends_ref, x, kappa)
        twos = [diffs[part] + weighted(terms, slopes(field, part, x, lane)[1]) for part in range(2)]
        pairs = [(ones[0], ones[0]), (ones[1], ones[1]), (twos[0], twos[0]), (twos[1], twos[1])]
        for left, right in ((ones, twos), (ones, diffs), (twos, diffs)):
            pairs += [(left[0], right[0]), (left[1], right[1]), (left[0], right[1]), (left[1], right[0])]
        for number, (left, right) in enumerate(pairs):
            totals[number] = totals[number] + fold(left * right)
    spot = lax.broadcasted_iota(jnp.int32, (1, 128), 1)
    row = jnp.zeros((1, 128), f32)
    for number in range(16):
        row = row + jnp.where(spot == number, jnp.sum(totals[number], keepdims=True), 0.0)
    out_ref[...] = jnp.broadcast_to(row, (DEVS, 128))


def leave_kernel(in_ref, z_ref, out_hbm, out_ref, sems):
    copies = [pltpu.make_async_copy(out_ref.at[x], out_hbm.at[0, x], sems.at[x]) for x in range(8)]
    for x in range(8):
        columns = []
        for yh in range(2):
            rows = [in_ref[pl.ds(block * 8 * 16 + yh * 8 + x, 8, stride=16), :] for block in range(16)]
            columns.append(jnp.concatenate(rows, axis=0))
        value = left_mul(z_ref, jnp.concatenate(columns, axis=1))
        out_ref[x] = value.T
        copies[x].start()
    for copy in copies:
        copy.wait()


def exchange(rows):
    wide = rows.reshape(rows.shape[0], 1, 128)
    return lax.all_to_all(wide, BOTH, split_axis=0, concat_axis=0, tiled=True).reshape(rows.shape)


def call(kernel, outs, scalars, scratch, *args, far_in=(), far_out=()):
    args = [
        pltpu.with_memory_space_constraint(arg, pltpu.HBM) if number in far_in else arg
        for number, arg in enumerate(args)
    ]
    outs = [pltpu.HBM(out.shape, out.dtype) if number in far_out else out for number, out in enumerate(outs)]
    return pl.pallas_call(
        kernel,
        out_shape=outs,
        in_specs=[
            smem() if number < scalars else (hbm() if number in far_in else vmem()) for number in range(len(args))
        ],
        out_specs=[hbm() if number in far_out else vmem() for number in range(len(outs))],
        scratch_shapes=scratch,
        name=kernel.__name__,
        compiler_params=pltpu.CompilerParams(vmem_limit_bytes=16 << 20),
    )(*args)


def shards(source, initial, diffusivity):
    table = tables()
    position = lax.axis_index("tm")
    slab = lax.axis_index("space")
    wave = (position * SLABS + slab).astype(f32)
    symbol_z = (4.0 * jnp.sin(math.pi * wave / NZ) ** 2).reshape(1)
    place = position.astype(jnp.int32).reshape(1)
    source, place, symbol_z = lax.optimization_barrier((source, place, symbol_z))

    slab_block = pltpu.VMEM((8, NY, NZ), f32)
    (rows,) = call(
        enter_kernel,
        [shape(DEVS * 17, 128)],
        1,
        [
            slab_block,
            slab_block,
            pltpu.VMEM((2, NY, NZ), f32),
            pltpu.VMEM((128, NZ), f32),
            pltpu.VMEM((2, NZ, NZ), bf16),
            pltpu.SemaphoreType.DMA((19,)),
        ],
        place,
        source[0],
        initial,
        diffusivity,
        table["z"],
        far_in=(1, 2, 3, 4),
    )
    rows = exchange(rows)
    big = pltpu.VMEM((1024, NY), f32)
    hat_one, rows, kappa = call(
        spectral_first_kernel,
        [shape(1024, NY), shape(DEVS * ROWS_FIRST, 128), shape(8, 128)],
        1,
        [big, big],
        symbol_z,
        rows,
        table["spectral"],
        table["symbol"],
    )
    rows, diffusivity = lax.optimization_barrier((rows, diffusivity))
    (faces,) = call(faces_kernel, [shape(41, NZ, 128)], 1, [], place, diffusivity)
    rows, faces = lax.optimization_barrier((rows, faces))
    rows = exchange(rows)
    block = pltpu.VMEM((21, NZ, 128), f32)
    rows, differ, right, ends = call(
        block_first_kernel,
        [shape(DEVS * 16, 128), shape(2, 8, NZ, 128), shape(2, 8, NZ, 128), shape(2, NZ, 128)],
        1,
        [block],
        place,
        kappa,
        rows,
        table["z"],
        faces,
    )
    rows = exchange(rows)
    hat_two, rows = call(
        spectral_second_kernel,
        [shape(1024, NY), shape(DEVS * ROWS, 128)],
        1,
        [big, big],
        symbol_z,
        kappa,
        rows,
        table["spectral"],
        table["symbol"],
    )
    rows = exchange(rows)
    (sums,) = call(block_second_kernel, [shape(DEVS, 128)], 0, [block], kappa, rows, differ, right, table["z"], faces, ends)
    sums, hat_one, hat_two = lax.optimization_barrier((sums, hat_one, hat_two))
    sums = exchange(sums)
    one, two = call(
        unfold_kernel, [shape(1024, NY), shape(1024, NY)], 0, [big], hat_one, hat_two, table["x"], table["y"]
    )
    (rows,) = call(combine_kernel, [shape(DEVS * 16, 128)], 0, [], sums, one, two)
    rows = exchange(rows)
    (field,) = call(
        leave_kernel,
        [shape(1, 8, NY, NZ)],
        0,
        [slab_block, pltpu.SemaphoreType.DMA((8,))],
        rows,
        table["z"],
        far_out=(0,),
    )
    return field


def solution(mesh):
    in_specs = (P("tm", "space", None, None), P("space", None, None), P("space", None, None))
    out_specs = P("tm", "space", None, None)
    return jax.shard_map(shards, mesh=mesh, in_specs=in_specs, out_specs=out_specs, check_vma=False)
```

```python
import functools
import math

import jax
import jax.numpy as jnp
import numpy as np
from jax import lax
from jax.experimental import pallas as pl
from jax.experimental.pallas import tpu as pltpu
from jax.sharding import PartitionSpec as P


alpha_corner = 0.05
step_length = 1.0
BOTH = ("tm", "space")
NX, NY, NZ = 128, 256, 128
STEPS = 8
ROWS = 21
COLUMN = NZ + 16
CHUNK = 16
ROWS_FIRST = 23
SLABS = 16
DEVS = 128
GROUPS = ((0, 1), (1, 3), (3, 8))
f32 = jnp.float32
bf16 = jnp.bfloat16
ROOT = alpha_corner ** (1.0 / STEPS)
HALF = math.sqrt(0.5)


def cas_table(length):
    index = np.arange(length)
    phase = (index[:, None] * index[None, :] % length) * (2.0 * np.pi / length)
    return (np.cos(phase) + np.sin(phase)) / math.sqrt(length)


def halves(table):
    table = np.asarray(table, np.float32)
    high = table.astype(bf16)
    low = (table - high.astype(np.float32)).astype(bf16)
    return np.stack([high, low])


def symbol_row(length):
    return 4.0 * np.sin(np.pi * np.arange(length) / length) ** 2


def tables():
    cas_x, cas_y, cas_z = cas_table(NX), cas_table(NY), cas_table(NZ)
    row = np.arange(NX)
    gathered = 8 * (row % 16) + row // 16
    row = np.arange(10 * 16)
    spread = (8 * (row % 16) + row // 16 - 1) % NX
    x_in, x_spread, y = halves(cas_x[:, gathered]), halves(cas_x[spread, :]), halves(cas_y)
    y_rows = [y[part, :, half * 128 : half * 128 + 128] for part in range(2) for half in range(2)]
    return {
        "spectral": np.concatenate([x_in[0], x_in[1], x_spread[0], x_spread[1], *y_rows]),
        "x": halves(cas_x),
        "y": y,
        "z": halves(cas_z),
        "symbol": np.asarray(symbol_row(NX)[:, None] + symbol_row(NY)[None, :], np.float32),
    }


def shift_of(frequency):
    phase = 2.0 * math.pi * frequency / STEPS
    return (1.0 - ROOT * math.cos(phase), ROOT * math.sin(phase) if frequency % 4 else 0.0)


def split(value):
    high = value.astype(bf16)
    return high, (value - high.astype(f32)).astype(bf16)


def dot(left, right):
    return jnp.dot(left, right, preferred_element_type=f32)


def left_mul(table, value):
    high, low = split(value)
    return dot(jnp.concatenate([table[0], table[1], table[0]], axis=1), jnp.concatenate([high, high, low], axis=0))


def right_mul(value, table):
    high, low = split(value)
    return dot(jnp.concatenate([high, high, low], axis=1), jnp.concatenate([table[0], table[1], table[0]], axis=0))


def spectral_parts(table_ref):
    x_in = table_ref[0:128, :], table_ref[128:256, :]
    x_spread = table_ref[256:416, :], table_ref[416:576, :]
    y = [
        jnp.concatenate([table_ref[row : row + 256, :], table_ref[row + 256 : row + 512, :]], axis=1)
        for row in (576, 1088)
    ]
    return x_in, x_spread, y


def vmem():
    return pl.BlockSpec(memory_space=pltpu.VMEM)


def smem():
    return pl.BlockSpec(memory_space=pltpu.SMEM)


def hbm():
    return pl.BlockSpec(memory_space=pltpu.HBM)


def shape(*dims):
    return jax.ShapeDtypeStruct(dims, f32)


def enter_kernel(
    place_ref,
    source_hbm,
    initial_hbm,
    kappa_hbm,
    z_hbm,
    out_ref,
    source_ref,
    initial_ref,
    kappa_ref,
    rim_ref,
    z_ref,
    sems,
):
    position = place_ref[0]
    first = jnp.where(position == 0, jnp.float32(1.0), jnp.float32(0.0))
    quarter = lax.rem(position, 4)
    half = pl.ds(pl.multiple_of(lax.rem(position, 2) * 128, 128), 128)
    table_copy = pltpu.make_async_copy(z_hbm, z_ref, sems.at[16])
    kappa_copy = pltpu.make_async_copy(kappa_hbm.at[pl.ds(2 * quarter, 2)], kappa_ref, sems.at[17])
    rim_copy = pltpu.make_async_copy(kappa_hbm.at[7 * (quarter // 2), half], rim_ref, sems.at[18])
    copies, added = [], []
    for number, (begin, end) in enumerate(GROUPS):
        planes = pl.ds(begin, end - begin)
        copies.append(pltpu.make_async_copy(source_hbm.at[planes], source_ref.at[planes], sems.at[number]))
        added.append(pltpu.make_async_copy(initial_hbm.at[planes], initial_ref.at[planes], sems.at[8 + number]))
    copies[0].start()
    added[0].start()
    table_copy.start()
    for copy, other in zip(copies[1:], added[1:]):
        copy.start()
        other.start()
    kappa_copy.start()
    rim_copy.start()
    table_copy.wait()
    nt = (((1,), (1,)), ((), ()))
    dims = functools.partial(lax.dot_general, dimension_numbers=nt, preferred_element_type=f32)
    z_wide = jnp.concatenate([z_ref[0], z_ref[1], z_ref[0]], axis=1)
    starts = {begin: number for number, (begin, _) in enumerate(GROUPS)}
    for x in range(8):
        if x in starts:
            copies[starts[x]].wait()
            added[starts[x]].wait()
        high, low = split(source_ref[x] + first * initial_ref[x])
        freq = dims(z_wide, jnp.concatenate([high, high, low], axis=1))
        for yh in range(2):
            for block in range(16):
                out_ref[pl.ds(block * 8 * 17 + yh * 8 + x, 8, stride=17), :] = freq[
                    block * 8 : block * 8 + 8, yh * 128 : yh * 128 + 128
                ]
    kappa_copy.wait()
    rim_copy.wait()
    total = jnp.sum(kappa_ref[...].reshape(64, 8, 128), axis=0)
    whole = jnp.broadcast_to(jnp.sum(total, keepdims=True), (8, 128))
    rim = rim_ref[...].T
    for block in range(16):
        out_ref[pl.ds(block * 8 * 17 + 16, 8, stride=17), :] = jnp.where(
            position < 4, rim[block * 8 : block * 8 + 8], whole
        )


def precondition_fields(work, kappa, symbol_z, symbol_ref, out):
    symbol = symbol_ref[...] + symbol_z
    scaled = step_length * kappa * symbol
    for pair in range(4):
        first = work[pl.ds(pair * 256, 128), :]
        second = work[pl.ds(pair * 256 + 128, 128), :]
        if pair == 0:
            out[pl.ds(0, 128), :] = first / (shift_of(0)[0] + scaled)
            out[pl.ds(128, 128), :] = second / (shift_of(4)[0] + scaled)
        else:
            shift = shift_of(pair)
            denom = shift[0] + scaled
            inverse = 1.0 / (denom * denom + shift[1] * shift[1])
            real, imag = denom * inverse, shift[1] * inverse
            out[pl.ds(pair * 256, 128), :] = first * real + second * imag
            out[pl.ds(pair * 256 + 128, 128), :] = second * real - first * imag


def spectral_core(
    kappa, symbol_z, gathered, table_ref, symbol_ref, hat_ref, out_ref, work, count
):
    x_in_ref, x_spread_ref, y_ref = spectral_parts(table_ref)
    for field in range(8):
        work[pl.ds(field * 128, 128), :] = left_mul(x_in_ref, gathered[pl.ds(field * 128, 128), :])
    work[...] = right_mul(work[...], y_ref)
    precondition_fields(work, kappa, symbol_z, symbol_ref, hat_ref)
    work[...] = right_mul(hat_ref[...], y_ref)
    lane = lax.broadcasted_iota(jnp.int32, (8, 128), 1)
    for pair in range(4):
        edges = {}
        for part in range(2):
            spread = left_mul(x_spread_ref, work[pl.ds((pair * 2 + part) * 128, 128), :])
            for core in range(2):
                for block in range(2):
                    base = ((2 * pair + core) * 16 + block * 8) * count
                    edge = edges.get((core, block), jnp.zeros((8, 128), f32))
                    for x in range(10):
                        rows = spread[x * 16 + block * 8 : x * 16 + block * 8 + 8]
                        out_ref[pl.ds(base + part * 10 + x, 8, stride=count), :] = rows[:, core * 128 : core * 128 + 128]
                        if 1 <= x <= 8:
                            spot = 2 * (part * 8 + x - 1)
                            other = rows[:, (1 - core) * 128 : (1 - core) * 128 + 128]
                            edge = jnp.where(lane // 2 == spot // 2, pltpu.roll(other, spot + 1, 1), edge)
                    edges[core, block] = edge
        for core in range(2):
            for block in range(2):
                base = ((2 * pair + core) * 16 + block * 8) * count
                out_ref[pl.ds(base + 20, 8, stride=count), :] = edges[core, block]


def spectral_first_kernel(
    symbol_z_ref,
    in_ref,
    table_ref,
    symbol_ref,
    hat_ref,
    out_ref,
    kappa_ref,
    gathered,
    work,
):

    def extra(step, block):
        return in_ref[pl.ds((step * 16 + block * 8) * 17 + 16, 8, stride=17), :]

    row = lax.broadcasted_iota(jnp.int32, (8, 128), 0)
    for core in range(2):
        first, last = [extra(core, 0), extra(core, 1)], [extra(2 + core, 0), extra(2 + core, 1)]
        for block in range(2):
            low = jnp.where(row == 0, pltpu.roll(last[1 - block], 1, 0), pltpu.roll(last[block], 1, 0))
            high = jnp.where(row == 7, pltpu.roll(first[1 - block], 7, 0), pltpu.roll(first[block], 7, 0))
            for pair in range(4):
                base = ((2 * pair + core) * 16 + block * 8) * ROWS_FIRST
                out_ref[pl.ds(base + 21, 8, stride=ROWS_FIRST), :] = low
                out_ref[pl.ds(base + 22, 8, stride=ROWS_FIRST), :] = high
    parts = extra(4, 0) + extra(4, 1)
    for step in range(5, 8):
        parts = parts + (extra(step, 0) + extra(step, 1))
    kappa = jnp.sum(parts, axis=0, keepdims=True) * (1.0 / (NX * NY * NZ))
    kappa_ref[...] = jnp.broadcast_to(kappa, (8, 128))
    kappa = kappa[:, 0:1]
    for x in range(8):
        for block in range(2):
            for yh in range(2):
                lifted = []
                for step in range(8):
                    row = (step * 16 + block * 8) * 17 + yh * 8 + x
                    lifted.append(in_ref[pl.ds(row, 8, stride=17), :] * (alpha_corner ** (step / STEPS)))
                plus = [lifted[m] + lifted[m + 4] for m in range(4)]
                minus = [lifted[m] - lifted[m + 4] for m in range(4)]
                odd_minus = HALF * (minus[1] - minus[3])
                odd_plus = HALF * (minus[1] + minus[3])
                even, odd = plus[0] + plus[2], plus[1] + plus[3]
                fields = [
                    even + odd,
                    even - odd,
                    minus[0] + odd_minus,
                    -minus[2] - odd_plus,
                    plus[0] - plus[2],
                    plus[3] - plus[1],
                    minus[0] - odd_minus,
                    minus[2] - odd_plus,
                ]
                for field in range(8):
                    gathered[pl.ds(field * 128 + x * 16 + block * 8, 8), pl.ds(yh * 128, 128)] = fields[field]
    spectral_core(
        kappa, symbol_z_ref[0], gathered, table_ref, symbol_ref, hat_ref, out_ref, work, ROWS_FIRST
    )


def spectral_second_kernel(
    symbol_z_ref, kappa_ref, in_ref, table_ref, symbol_ref, hat_ref, out_ref, gathered, work
):
    for field in range(8):
        pair, part = field // 2, field % 2
        for core in range(2):
            for x in range(8):
                for block in range(2):
                    row = ((2 * pair + core) * 16 + block * 8) * 16 + part * 8 + x
                    gathered[pl.ds(field * 128 + x * 16 + block * 8, 8), pl.ds(core * 128, 128)] = in_ref[
                        pl.ds(row, 8, stride=16), :
                    ]
    kappa = kappa_ref[0:1, 0:1]
    spectral_core(
        kappa, symbol_z_ref[0], gathered, table_ref, symbol_ref, hat_ref, out_ref, work, ROWS
    )


def coefficients(sums):
    lane = lax.broadcasted_iota(jnp.int32, (4, 128), 1)

    def pick(number):
        return jnp.sum(jnp.where(lane == number, sums, 0.0), axis=1, keepdims=True)

    values = [pick(number) for number in range(16)]
    packed = lax.broadcasted_iota(jnp.int32, (4, 1), 0) == 0

    def complex_of(base):
        return values[base] + values[base + 1], values[base + 2] - values[base + 3]

    def solve(g11, g22, g12, h1, h2):
        scale1 = jnp.where(g11 > 0.0, lax.rsqrt(jnp.maximum(g11, 1e-37)), 0.0)
        scale2 = jnp.where(g22 > 0.0, lax.rsqrt(jnp.maximum(g22, 1e-37)), 0.0)
        corr = (g12[0] * scale1 * scale2, g12[1] * scale1 * scale2)
        t1 = (h1[0] * scale1, h1[1] * scale1)
        t2 = (h2[0] * scale2, h2[1] * scale2)
        det = 1.0 - (corr[0] * corr[0] + corr[1] * corr[1])
        good = jnp.logical_and(det > 1e-6, g22 > 0.0)
        inv = jnp.where(good, 1.0 / jnp.where(good, det, 1.0), 0.0)
        one = (
            jnp.where(good, (t1[0] - (corr[0] * t2[0] - corr[1] * t2[1])) * inv, t1[0]),
            jnp.where(good, (t1[1] - (corr[0] * t2[1] + corr[1] * t2[0])) * inv, t1[1]),
        )
        two = (
            (t2[0] - (corr[0] * t1[0] + corr[1] * t1[1])) * inv,
            (t2[1] - (corr[0] * t1[1] - corr[1] * t1[0])) * inv,
        )
        return (1.0 - one[0] * scale1, -one[1] * scale1), (-two[0] * scale2, -two[1] * scale2)

    zero = jnp.zeros((4, 1), f32)
    full = solve(values[0] + values[1], values[2] + values[3], complex_of(4), complex_of(8), complex_of(12))
    first = solve(values[0], values[2], (values[4], zero), (values[8], zero), (values[12], zero))
    second = solve(values[1], values[3], (values[5], zero), (values[9], zero), (values[13], zero))
    maps = []
    for vector in range(2):
        maps.append(
            (
                jnp.where(packed, first[vector][0], full[vector][0]),
                jnp.where(packed, 0.0, full[vector][1]),
                jnp.where(packed, second[vector][0], full[vector][0]),
            )
        )
    return maps


def unfold_kernel(hat_one_ref, hat_two_ref, x_ref, y_ref, one_ref, two_ref, work):
    for hat, out in ((hat_one_ref, one_ref), (hat_two_ref, two_ref)):
        work[...] = right_mul(hat[...], y_ref)
        for field in range(8):
            rows = pl.ds(field * 128, 128)
            out[rows, :] = left_mul(x_ref, work[rows, :])


def combine_kernel(sums_ref, one_ref, two_ref, out_ref):
    sums = jnp.concatenate(
        [jnp.sum(sums_ref[pl.ds(pair * 32, 32), :], axis=0, keepdims=True) for pair in range(4)], axis=0
    )
    maps = coefficients(sums)
    scales = [
        [[jnp.broadcast_to(entry[pair : pair + 1, :], (8, NY)) for entry in vector] for pair in range(4)]
        for vector in maps
    ]
    for slab in range(16):
        fields = []
        for pair in range(4):
            parts = []
            for ref in (one_ref, two_ref):
                row = pair * 256 + slab * 8
                parts.append((ref[pl.ds(row, 8), :], ref[pl.ds(row + 128, 8), :]))
            (p1, q1), (p2, q2) = parts
            (a1, b1, c1), (a2, b2, c2) = scales[0][pair], scales[1][pair]
            fields.append(a1 * p1 - b1 * q1 + (a2 * p2 - b2 * q2))
            fields.append(c1 * q1 + b1 * p1 + (c2 * q2 + b2 * p2))
        zero, four, re1, im1, re2, im2, re3, im3 = fields
        even = [zero + four + 2.0 * re2, zero - four - 2.0 * im2, zero + four - 2.0 * re2, zero - four + 2.0 * im2]
        diff, total = (2.0 * HALF) * (re1 - re3), (2.0 * HALF) * (im1 + im3)
        odd = [2.0 * (re1 + re3), diff - total, 2.0 * (im3 - im1), -diff - total]
        for step in range(8):
            value = even[step % 4] + odd[step % 4] if step < 4 else even[step % 4] - odd[step % 4]
            value = value * (alpha_corner ** (-step / STEPS) / STEPS)
            for yh in range(2):
                out_ref[pl.ds((step * 16 + slab) * 16 + yh * 8, 8), :] = value[:, yh * 128 : yh * 128 + 128]


def faces_kernel(place_ref, kappa_ref, faces_ref):
    upper = lax.rem(place_ref[0], 2) == 1

    def half(plane):
        return jnp.where(upper, plane[128:], plane[:128]).T

    before = None
    for x in range(8):
        whole = kappa_ref[x]
        here = half(whole)
        faces_ref[9 + x] = 0.5 * (here + half(pltpu.roll(whole, NY - 1, 0)))
        faces_ref[17 + x] = 0.5 * (here + half(pltpu.roll(whole, 1, 0)))
        faces_ref[25 + x] = 0.5 * (here + pltpu.roll(here, NZ - 1, 0))
        faces_ref[33 + x] = 0.5 * (here + pltpu.roll(here, 1, 0))
        if x == 0:
            faces_ref[0] = here
        else:
            faces_ref[x] = 0.5 * (before + here)
        before = here
    faces_ref[8] = before


def column(in_ref, number, count):
    return jnp.concatenate(
        [in_ref[pl.ds(block * 8 * count + number, 8, stride=count), :] for block in range(16)], axis=0
    )


def load_block(in_ref, z_ref, field, count):
    def put(number, value):
        base = number * COLUMN + 8
        field[base : base + NZ, :] = value
        field[base - 1 : base, :] = value[NZ - 1 : NZ, :]
        field[base + NZ : base + NZ + 1, :] = value[0:1, :]

    for number in range(0, 20, 2):
        columns = [column(in_ref, number + step, count) for step in range(2)]
        both = left_mul(z_ref, jnp.concatenate(columns, axis=1))
        put(number, both[:, :128])
        put(number + 1, both[:, 128:])
    put(20, left_mul(z_ref, column(in_ref, 20, count)))


def slopes(field, part, x, z, lane):
    def rows(number, step=0):
        return field[pl.ds(number * COLUMN + 8 + z + step, CHUNK), :]

    number = part * 10 + x + 1
    here, edge = rows(number), rows(20)
    spot = 2 * (part * 8 + x)
    below = jnp.where(lane == 0, pltpu.roll(edge, (128 - spot) % 128, 1), pltpu.roll(here, 1, 1))
    above = jnp.where(lane == 127, pltpu.roll(edge, 126 - spot, 1), pltpu.roll(here, 127, 1))
    others = [rows(number - 1), rows(number + 1), above, below, rows(number, 1), rows(number, -1)]
    return here, [here - other for other in others]


def weights(faces_ref, ends_ref, x, z, kappa):
    rows = pl.ds(z, CHUNK)
    low = ends_ref[0, rows, :] if x == 0 else faces_ref[x, rows, :]
    high = ends_ref[1, rows, :] if x == 7 else faces_ref[x + 1, rows, :]
    terms = [low, high] + [faces_ref[8 * number + 1 + x, rows, :] for number in range(1, 5)]
    return [term - kappa for term in terms]


def weighted(terms, values):
    total = [term * value for term, value in zip(terms, values)]
    return ((total[0] + total[1]) + (total[2] + total[3])) + (total[4] + total[5])


def block_first_kernel(place_ref, kappa_ref, in_ref, z_ref, faces_ref, out_ref, differ_ref, right_ref, ends_ref, field):
    kappa = kappa_ref[0:1, 0:1]
    pair = place_ref[0] // 2
    real = [jnp.float32(shift_of(4 * part)[0]) for part in range(2)]
    imag = jnp.float32(0.0)
    for number in range(1, 4):
        real = [jnp.where(pair == number, shift_of(number)[0], value) for value in real]
        imag = jnp.where(pair == number, shift_of(number)[1], imag)
    load_block(in_ref, z_ref, field, ROWS_FIRST)
    ends_ref[0] = 0.5 * (column(in_ref, 21, ROWS_FIRST) + faces_ref[0])
    ends_ref[1] = 0.5 * (column(in_ref, 22, ROWS_FIRST) + faces_ref[8])
    lane = lax.broadcasted_iota(jnp.int32, (CHUNK, 128), 1)
    for x in range(8):
        for z in range(0, NZ, CHUNK):
            terms = weights(faces_ref, ends_ref, x, z, kappa)
            cells = [slopes(field, part, x, z, lane) for part in range(2)]
            for part in range(2):
                here, slope = cells[part]
                differ_ref[part, x, pl.ds(z, CHUNK), :] = weighted(terms, slope)
                cross = -imag if part == 0 else imag
                right_ref[part, x, pl.ds(z, CHUNK), :] = (
                    real[part] * here
                    + cross * cells[1 - part][0]
                    + (step_length * kappa)
                    * (((slope[0] + slope[1]) + (slope[2] + slope[3])) + (slope[4] + slope[5]))
                )
        freq = left_mul(z_ref, jnp.concatenate([differ_ref[0, x], differ_ref[1, x]], axis=1))
        for part in range(2):
            for block in range(16):
                out_ref[pl.ds(block * 8 * 16 + part * 8 + x, 8, stride=16), :] = freq[
                    block * 8 : block * 8 + 8, part * 128 : part * 128 + 128
                ]


def block_second_kernel(
    kappa_ref, in_ref, differ_ref, right_ref, z_ref, faces_ref, ends_ref, out_ref, field
):
    kappa = kappa_ref[0:1, 0:1]
    load_block(in_ref, z_ref, field, ROWS)
    lane = lax.broadcasted_iota(jnp.int32, (CHUNK, 128), 1)
    totals = [jnp.zeros((8, 128), f32) for _ in range(16)]

    def fold(value):
        return jnp.sum(value.reshape(CHUNK // 8, 8, 128), axis=0)

    for x in range(8):
        for z in range(0, NZ, CHUNK):
            terms = weights(faces_ref, ends_ref, x, z, kappa)
            diffs = [differ_ref[part, x, pl.ds(z, CHUNK), :] for part in range(2)]
            ones = [right_ref[part, x, pl.ds(z, CHUNK), :] + diffs[part] for part in range(2)]
            twos = [diffs[part] + weighted(terms, slopes(field, part, x, z, lane)[1]) for part in range(2)]
            pairs = [(ones[0], ones[0]), (ones[1], ones[1]), (twos[0], twos[0]), (twos[1], twos[1])]
            for left, right in ((ones, twos), (ones, diffs), (twos, diffs)):
                pairs += [(left[0], right[0]), (left[1], right[1]), (left[0], right[1]), (left[1], right[0])]
            for number, (left, right) in enumerate(pairs):
                totals[number] = totals[number] + fold(left * right)
    spot = lax.broadcasted_iota(jnp.int32, (1, 128), 1)
    row = jnp.zeros((1, 128), f32)
    for number in range(16):
        row = row + jnp.where(spot == number, jnp.sum(totals[number], keepdims=True), 0.0)
    out_ref[...] = jnp.broadcast_to(row, (DEVS, 128))


def leave_kernel(in_ref, z_ref, out_hbm, out_ref, sems):
    copies = [pltpu.make_async_copy(out_ref.at[x], out_hbm.at[0, x], sems.at[x]) for x in range(8)]
    for x in range(8):
        columns = []
        for yh in range(2):
            rows = [in_ref[pl.ds(block * 8 * 16 + yh * 8 + x, 8, stride=16), :] for block in range(16)]
            columns.append(jnp.concatenate(rows, axis=0))
        value = left_mul(z_ref, jnp.concatenate(columns, axis=1))
        out_ref[x] = value.T
        copies[x].start()
    for copy in copies:
        copy.wait()


def exchange(rows):
    wide = rows.reshape(rows.shape[0], 1, 128)
    return lax.all_to_all(wide, BOTH, split_axis=0, concat_axis=0, tiled=True).reshape(rows.shape)


def call(kernel, outs, scalars, scratch, *args, far_in=(), far_out=()):
    args = [
        pltpu.with_memory_space_constraint(arg, pltpu.HBM) if number in far_in else arg
        for number, arg in enumerate(args)
    ]
    outs = [pltpu.HBM(out.shape, out.dtype) if number in far_out else out for number, out in enumerate(outs)]
    return pl.pallas_call(
        kernel,
        out_shape=outs,
        in_specs=[
            smem() if number < scalars else (hbm() if number in far_in else vmem()) for number in range(len(args))
        ],
        out_specs=[hbm() if number in far_out else vmem() for number in range(len(outs))],
        scratch_shapes=scratch,
        name=kernel.__name__,
        compiler_params=pltpu.CompilerParams(vmem_limit_bytes=16 << 20),
    )(*args)


def shards(source, initial, diffusivity):
    table = tables()
    position = lax.axis_index("tm")
    slab = lax.axis_index("space")
    wave = (position * SLABS + slab).astype(f32)
    symbol_z = (4.0 * jnp.sin(math.pi * wave / NZ) ** 2).reshape(1)
    place = position.astype(jnp.int32).reshape(1)
    source, place, symbol_z = lax.optimization_barrier((source, place, symbol_z))

    slab_block = pltpu.VMEM((8, NY, NZ), f32)
    (rows,) = call(
        enter_kernel,
        [shape(DEVS * 17, 128)],
        1,
        [
            slab_block,
            slab_block,
            pltpu.VMEM((2, NY, NZ), f32),
            pltpu.VMEM((128, NZ), f32),
            pltpu.VMEM((2, NZ, NZ), bf16),
            pltpu.SemaphoreType.DMA((19,)),
        ],
        place,
        source[0],
        initial,
        diffusivity,
        table["z"],
        far_in=(1, 2, 3, 4),
    )
    rows = exchange(rows)
    big = pltpu.VMEM((1024, NY), f32)
    hat_one, rows, kappa = call(
        spectral_first_kernel,
        [shape(1024, NY), shape(DEVS * ROWS_FIRST, 128), shape(8, 128)],
        1,
        [big, big],
        symbol_z,
        rows,
        table["spectral"],
        table["symbol"],
    )
    rows, diffusivity = lax.optimization_barrier((rows, diffusivity))
    (faces,) = call(faces_kernel, [shape(41, NZ, 128)], 1, [], place, diffusivity)
    rows, faces = lax.optimization_barrier((rows, faces))
    rows = exchange(rows)
    block = pltpu.VMEM((21 * COLUMN, 128), f32)
    rows, differ, right, ends = call(
        block_first_kernel,
        [shape(DEVS * 16, 128), shape(2, 8, NZ, 128), shape(2, 8, NZ, 128), shape(2, NZ, 128)],
        1,
        [block],
        place,
        kappa,
        rows,
        table["z"],
        faces,
    )
    rows = exchange(rows)
    hat_two, rows = call(
        spectral_second_kernel,
        [shape(1024, NY), shape(DEVS * ROWS, 128)],
        1,
        [big, big],
        symbol_z,
        kappa,
        rows,
        table["spectral"],
        table["symbol"],
    )
    rows = exchange(rows)
    (sums,) = call(block_second_kernel, [shape(DEVS, 128)], 0, [block], kappa, rows, differ, right, table["z"], faces, ends)
    sums, hat_one, hat_two = lax.optimization_barrier((sums, hat_one, hat_two))
    sums = exchange(sums)
    one, two = call(
        unfold_kernel, [shape(1024, NY), shape(1024, NY)], 0, [big], hat_one, hat_two, table["x"], table["y"]
    )
    (rows,) = call(combine_kernel, [shape(DEVS * 16, 128)], 0, [], sums, one, two)
    rows = exchange(rows)
    (field,) = call(
        leave_kernel,
        [shape(1, 8, NY, NZ)],
        0,
        [slab_block, pltpu.SemaphoreType.DMA((8,))],
        rows,
        table["z"],
        far_out=(0,),
    )
    return field


def solution(mesh):
    in_specs = (P("tm", "space", None, None), P("space", None, None), P("space", None, None))
    out_specs = P("tm", "space", None, None)
    return jax.shard_map(shards, mesh=mesh, in_specs=in_specs, out_specs=out_specs, check_vma=False)
```

```python
import functools
import math

import jax
import jax.numpy as jnp
import numpy as np
from jax import lax
from jax.experimental import pallas as pl
from jax.experimental.pallas import tpu as pltpu
from jax.sharding import PartitionSpec as P


alpha_corner = 0.05
step_length = 1.0
BOTH = ("tm", "space")
NX, NY, NZ = 128, 256, 128
STEPS = 8
ROWS = 21
COLUMN = NZ + 16
CHUNK = 16
ROWS_FIRST = 23
SLABS = 16
DEVS = 128
GROUPS = ((0, 1), (1, 4), (4, 8))
f32 = jnp.float32
bf16 = jnp.bfloat16
ROOT = alpha_corner ** (1.0 / STEPS)
HALF = math.sqrt(0.5)


def cas_table(length):
    index = np.arange(length)
    phase = (index[:, None] * index[None, :] % length) * (2.0 * np.pi / length)
    return (np.cos(phase) + np.sin(phase)) / math.sqrt(length)


def halves(table):
    table = np.asarray(table, np.float32)
    high = table.astype(bf16)
    low = (table - high.astype(np.float32)).astype(bf16)
    return np.stack([high, low])


def symbol_row(length):
    return 4.0 * np.sin(np.pi * np.arange(length) / length) ** 2


def tables():
    cas_x, cas_y, cas_z = cas_table(NX), cas_table(NY), cas_table(NZ)
    row = np.arange(NX)
    gathered = 8 * (row % 16) + row // 16
    row = np.arange(10 * 16)
    spread = (8 * (row % 16) + row // 16 - 1) % NX
    x_in, x_spread, y = halves(cas_x[:, gathered]), halves(cas_x[spread, :]), halves(cas_y)
    y_rows = [y[part, :, half * 128 : half * 128 + 128] for part in range(2) for half in range(2)]
    return {
        "spectral": np.concatenate([x_in[0], x_in[1], x_spread[0], x_spread[1], *y_rows]),
        "x": halves(cas_x),
        "y": y,
        "z": halves(cas_z),
        "symbol": np.asarray(symbol_row(NX)[:, None] + symbol_row(NY)[None, :], np.float32),
    }


def shift_of(frequency):
    phase = 2.0 * math.pi * frequency / STEPS
    return (1.0 - ROOT * math.cos(phase), ROOT * math.sin(phase) if frequency % 4 else 0.0)


def split(value):
    high = value.astype(bf16)
    return high, (value - high.astype(f32)).astype(bf16)


def dot(left, right):
    return jnp.dot(left, right, preferred_element_type=f32)


def left_mul(table, value):
    high, low = split(value)
    return dot(jnp.concatenate([table[0], table[1], table[0]], axis=1), jnp.concatenate([high, high, low], axis=0))


def right_mul(value, table):
    high, low = split(value)
    return dot(jnp.concatenate([high, high, low], axis=1), jnp.concatenate([table[0], table[1], table[0]], axis=0))


def spectral_parts(table_ref):
    x_in = table_ref[0:128, :], table_ref[128:256, :]
    x_spread = table_ref[256:416, :], table_ref[416:576, :]
    y = [
        jnp.concatenate([table_ref[row : row + 256, :], table_ref[row + 256 : row + 512, :]], axis=1)
        for row in (576, 1088)
    ]
    return x_in, x_spread, y


def vmem():
    return pl.BlockSpec(memory_space=pltpu.VMEM)


def smem():
    return pl.BlockSpec(memory_space=pltpu.SMEM)


def hbm():
    return pl.BlockSpec(memory_space=pltpu.HBM)


def shape(*dims):
    return jax.ShapeDtypeStruct(dims, f32)


def enter_kernel(
    place_ref,
    source_hbm,
    initial_hbm,
    kappa_hbm,
    z_hbm,
    out_ref,
    source_ref,
    initial_ref,
    kappa_ref,
    rim_ref,
    z_ref,
    sems,
):
    position = place_ref[0]
    first = jnp.where(position == 0, jnp.float32(1.0), jnp.float32(0.0))
    quarter = lax.rem(position, 4)
    half = pl.ds(pl.multiple_of(lax.rem(position, 2) * 128, 128), 128)
    table_copy = pltpu.make_async_copy(z_hbm, z_ref, sems.at[16])
    kappa_copy = pltpu.make_async_copy(kappa_hbm.at[pl.ds(2 * quarter, 2)], kappa_ref, sems.at[17])
    rim_copy = pltpu.make_async_copy(kappa_hbm.at[7 * (quarter // 2), half], rim_ref, sems.at[18])
    copies, added = [], []
    for number, (begin, end) in enumerate(GROUPS):
        planes = pl.ds(begin, end - begin)
        copies.append(pltpu.make_async_copy(source_hbm.at[planes], source_ref.at[planes], sems.at[number]))
        added.append(pltpu.make_async_copy(initial_hbm.at[planes], initial_ref.at[planes], sems.at[8 + number]))
    copies[0].start()
    added[0].start()
    table_copy.start()
    for copy, other in zip(copies[1:], added[1:]):
        copy.start()
        other.start()
    kappa_copy.start()
    rim_copy.start()
    table_copy.wait()
    nt = (((1,), (1,)), ((), ()))
    dims = functools.partial(lax.dot_general, dimension_numbers=nt, preferred_element_type=f32)
    z_wide = jnp.concatenate([z_ref[0], z_ref[1], z_ref[0]], axis=1)
    starts = {begin: number for number, (begin, _) in enumerate(GROUPS)}
    for x in range(8):
        if x in starts:
            copies[starts[x]].wait()
            added[starts[x]].wait()
        high, low = split(source_ref[x] + first * initial_ref[x])
        freq = dims(z_wide, jnp.concatenate([high, high, low], axis=1))
        for yh in range(2):
            for block in range(16):
                out_ref[pl.ds(block * 8 * 17 + yh * 8 + x, 8, stride=17), :] = freq[
                    block * 8 : block * 8 + 8, yh * 128 : yh * 128 + 128
                ]
    kappa_copy.wait()
    rim_copy.wait()
    total = jnp.sum(kappa_ref[...].reshape(64, 8, 128), axis=0)
    whole = jnp.broadcast_to(jnp.sum(total, keepdims=True), (8, 128))
    rim = rim_ref[...].T
    for block in range(16):
        out_ref[pl.ds(block * 8 * 17 + 16, 8, stride=17), :] = jnp.where(
            position < 4, rim[block * 8 : block * 8 + 8], whole
        )


def precondition_fields(work, kappa, symbol_z, symbol_ref, out):
    symbol = symbol_ref[...] + symbol_z
    scaled = step_length * kappa * symbol
    for pair in range(4):
        first = work[pl.ds(pair * 256, 128), :]
        second = work[pl.ds(pair * 256 + 128, 128), :]
        if pair == 0:
            out[pl.ds(0, 128), :] = first / (shift_of(0)[0] + scaled)
            out[pl.ds(128, 128), :] = second / (shift_of(4)[0] + scaled)
        else:
            shift = shift_of(pair)
            denom = shift[0] + scaled
            inverse = 1.0 / (denom * denom + shift[1] * shift[1])
            real, imag = denom * inverse, shift[1] * inverse
            out[pl.ds(pair * 256, 128), :] = first * real + second * imag
            out[pl.ds(pair * 256 + 128, 128), :] = second * real - first * imag


def spectral_core(
    kappa, symbol_z, gathered, table_ref, symbol_ref, hat_ref, out_ref, work, count
):
    x_in_ref, x_spread_ref, y_ref = spectral_parts(table_ref)
    for field in range(8):
        work[pl.ds(field * 128, 128), :] = left_mul(x_in_ref, gathered[pl.ds(field * 128, 128), :])
    work[...] = right_mul(work[...], y_ref)
    precondition_fields(work, kappa, symbol_z, symbol_ref, hat_ref)
    work[...] = right_mul(hat_ref[...], y_ref)
    lane = lax.broadcasted_iota(jnp.int32, (8, 128), 1)
    for pair in range(4):
        edges = {}
        for part in range(2):
            spread = left_mul(x_spread_ref, work[pl.ds((pair * 2 + part) * 128, 128), :])
            for core in range(2):
                for block in range(2):
                    base = ((2 * pair + core) * 16 + block * 8) * count
                    edge = edges.get((core, block), jnp.zeros((8, 128), f32))
                    for x in range(10):
                        rows = spread[x * 16 + block * 8 : x * 16 + block * 8 + 8]
                        out_ref[pl.ds(base + part * 10 + x, 8, stride=count), :] = rows[:, core * 128 : core * 128 + 128]
                        if 1 <= x <= 8:
                            spot = 2 * (part * 8 + x - 1)
                            other = rows[:, (1 - core) * 128 : (1 - core) * 128 + 128]
                            edge = jnp.where(lane // 2 == spot // 2, pltpu.roll(other, spot + 1, 1), edge)
                    edges[core, block] = edge
        for core in range(2):
            for block in range(2):
                base = ((2 * pair + core) * 16 + block * 8) * count
                out_ref[pl.ds(base + 20, 8, stride=count), :] = edges[core, block]


def spectral_first_kernel(
    symbol_z_ref,
    in_ref,
    table_ref,
    symbol_ref,
    hat_ref,
    out_ref,
    kappa_ref,
    gathered,
    work,
):

    def extra(step, block):
        return in_ref[pl.ds((step * 16 + block * 8) * 17 + 16, 8, stride=17), :]

    row = lax.broadcasted_iota(jnp.int32, (8, 128), 0)
    for core in range(2):
        first, last = [extra(core, 0), extra(core, 1)], [extra(2 + core, 0), extra(2 + core, 1)]
        for block in range(2):
            low = jnp.where(row == 0, pltpu.roll(last[1 - block], 1, 0), pltpu.roll(last[block], 1, 0))
            high = jnp.where(row == 7, pltpu.roll(first[1 - block], 7, 0), pltpu.roll(first[block], 7, 0))
            for pair in range(4):
                base = ((2 * pair + core) * 16 + block * 8) * ROWS_FIRST
                out_ref[pl.ds(base + 21, 8, stride=ROWS_FIRST), :] = low
                out_ref[pl.ds(base + 22, 8, stride=ROWS_FIRST), :] = high
    parts = extra(4, 0) + extra(4, 1)
    for step in range(5, 8):
        parts = parts + (extra(step, 0) + extra(step, 1))
    kappa = jnp.sum(parts, axis=0, keepdims=True) * (1.0 / (NX * NY * NZ))
    kappa_ref[...] = jnp.broadcast_to(kappa, (8, 128))
    kappa = kappa[:, 0:1]
    for x in range(8):
        for block in range(2):
            for yh in range(2):
                lifted = []
                for step in range(8):
                    row = (step * 16 + block * 8) * 17 + yh * 8 + x
                    lifted.append(in_ref[pl.ds(row, 8, stride=17), :] * (alpha_corner ** (step / STEPS)))
                plus = [lifted[m] + lifted[m + 4] for m in range(4)]
                minus = [lifted[m] - lifted[m + 4] for m in range(4)]
                odd_minus = HALF * (minus[1] - minus[3])
                odd_plus = HALF * (minus[1] + minus[3])
                even, odd = plus[0] + plus[2], plus[1] + plus[3]
                fields = [
                    even + odd,
                    even - odd,
                    minus[0] + odd_minus,
                    -minus[2] - odd_plus,
                    plus[0] - plus[2],
                    plus[3] - plus[1],
                    minus[0] - odd_minus,
                    minus[2] - odd_plus,
                ]
                for field in range(8):
                    gathered[pl.ds(field * 128 + x * 16 + block * 8, 8), pl.ds(yh * 128, 128)] = fields[field]
    spectral_core(
        kappa, symbol_z_ref[0], gathered, table_ref, symbol_ref, hat_ref, out_ref, work, ROWS_FIRST
    )


def spectral_second_kernel(
    symbol_z_ref, kappa_ref, in_ref, table_ref, symbol_ref, hat_ref, out_ref, gathered, work
):
    for field in range(8):
        pair, part = field // 2, field % 2
        for core in range(2):
            for x in range(8):
                for block in range(2):
                    row = ((2 * pair + core) * 16 + block * 8) * 16 + part * 8 + x
                    gathered[pl.ds(field * 128 + x * 16 + block * 8, 8), pl.ds(core * 128, 128)] = in_ref[
                        pl.ds(row, 8, stride=16), :
                    ]
    kappa = kappa_ref[0:1, 0:1]
    spectral_core(
        kappa, symbol_z_ref[0], gathered, table_ref, symbol_ref, hat_ref, out_ref, work, ROWS
    )


def coefficients(sums):
    lane = lax.broadcasted_iota(jnp.int32, (4, 128), 1)

    def pick(number):
        return jnp.sum(jnp.where(lane == number, sums, 0.0), axis=1, keepdims=True)

    values = [pick(number) for number in range(16)]
    packed = lax.broadcasted_iota(jnp.int32, (4, 1), 0) == 0

    def complex_of(base):
        return values[base] + values[base + 1], values[base + 2] - values[base + 3]

    def solve(g11, g22, g12, h1, h2):
        scale1 = jnp.where(g11 > 0.0, lax.rsqrt(jnp.maximum(g11, 1e-37)), 0.0)
        scale2 = jnp.where(g22 > 0.0, lax.rsqrt(jnp.maximum(g22, 1e-37)), 0.0)
        corr = (g12[0] * scale1 * scale2, g12[1] * scale1 * scale2)
        t1 = (h1[0] * scale1, h1[1] * scale1)
        t2 = (h2[0] * scale2, h2[1] * scale2)
        det = 1.0 - (corr[0] * corr[0] + corr[1] * corr[1])
        good = jnp.logical_and(det > 1e-6, g22 > 0.0)
        inv = jnp.where(good, 1.0 / jnp.where(good, det, 1.0), 0.0)
        one = (
            jnp.where(good, (t1[0] - (corr[0] * t2[0] - corr[1] * t2[1])) * inv, t1[0]),
            jnp.where(good, (t1[1] - (corr[0] * t2[1] + corr[1] * t2[0])) * inv, t1[1]),
        )
        two = (
            (t2[0] - (corr[0] * t1[0] + corr[1] * t1[1])) * inv,
            (t2[1] - (corr[0] * t1[1] - corr[1] * t1[0])) * inv,
        )
        return (1.0 - one[0] * scale1, -one[1] * scale1), (-two[0] * scale2, -two[1] * scale2)

    zero = jnp.zeros((4, 1), f32)
    full = solve(values[0] + values[1], values[2] + values[3], complex_of(4), complex_of(8), complex_of(12))
    first = solve(values[0], values[2], (values[4], zero), (values[8], zero), (values[12], zero))
    second = solve(values[1], values[3], (values[5], zero), (values[9], zero), (values[13], zero))
    maps = []
    for vector in range(2):
        maps.append(
            (
                jnp.where(packed, first[vector][0], full[vector][0]),
                jnp.where(packed, 0.0, full[vector][1]),
                jnp.where(packed, second[vector][0], full[vector][0]),
            )
        )
    return maps


def unfold_kernel(hat_one_ref, hat_two_ref, x_ref, y_ref, one_ref, two_ref, work):
    for hat, out in ((hat_one_ref, one_ref), (hat_two_ref, two_ref)):
        work[...] = right_mul(hat[...], y_ref)
        for field in range(8):
            rows = pl.ds(field * 128, 128)
            out[rows, :] = left_mul(x_ref, work[rows, :])


def combine_kernel(sums_ref, one_ref, two_ref, out_ref):
    sums = jnp.concatenate(
        [jnp.sum(sums_ref[pl.ds(pair * 32, 32), :], axis=0, keepdims=True) for pair in range(4)], axis=0
    )
    maps = coefficients(sums)
    scales = [
        [[jnp.broadcast_to(entry[pair : pair + 1, :], (8, NY)) for entry in vector] for pair in range(4)]
        for vector in maps
    ]
    for slab in range(16):
        fields = []
        for pair in range(4):
            parts = []
            for ref in (one_ref, two_ref):
                row = pair * 256 + slab * 8
                parts.append((ref[pl.ds(row, 8), :], ref[pl.ds(row + 128, 8), :]))
            (p1, q1), (p2, q2) = parts
            (a1, b1, c1), (a2, b2, c2) = scales[0][pair], scales[1][pair]
            fields.append(a1 * p1 - b1 * q1 + (a2 * p2 - b2 * q2))
            fields.append(c1 * q1 + b1 * p1 + (c2 * q2 + b2 * p2))
        zero, four, re1, im1, re2, im2, re3, im3 = fields
        even = [zero + four + 2.0 * re2, zero - four - 2.0 * im2, zero + four - 2.0 * re2, zero - four + 2.0 * im2]
        diff, total = (2.0 * HALF) * (re1 - re3), (2.0 * HALF) * (im1 + im3)
        odd = [2.0 * (re1 + re3), diff - total, 2.0 * (im3 - im1), -diff - total]
        for step in range(8):
            value = even[step % 4] + odd[step % 4] if step < 4 else even[step % 4] - odd[step % 4]
            value = value * (alpha_corner ** (-step / STEPS) / STEPS)
            for yh in range(2):
                out_ref[pl.ds((step * 16 + slab) * 16 + yh * 8, 8), :] = value[:, yh * 128 : yh * 128 + 128]


def faces_kernel(place_ref, kappa_ref, faces_ref):
    upper = lax.rem(place_ref[0], 2) == 1

    def half(plane):
        return jnp.where(upper, plane[128:], plane[:128]).T

    before = None
    for x in range(8):
        whole = kappa_ref[x]
        here = half(whole)
        faces_ref[9 + x] = 0.5 * (here + half(pltpu.roll(whole, NY - 1, 0)))
        faces_ref[17 + x] = 0.5 * (here + half(pltpu.roll(whole, 1, 0)))
        faces_ref[25 + x] = 0.5 * (here + pltpu.roll(here, NZ - 1, 0))
        faces_ref[33 + x] = 0.5 * (here + pltpu.roll(here, 1, 0))
        if x == 0:
            faces_ref[0] = here
        else:
            faces_ref[x] = 0.5 * (before + here)
        before = here
    faces_ref[8] = before


def column(in_ref, number, count):
    return jnp.concatenate(
        [in_ref[pl.ds(block * 8 * count + number, 8, stride=count), :] for block in range(16)], axis=0
    )


def load_block(in_ref, z_ref, field, count):
    def put(number, value):
        base = number * COLUMN + 8
        field[base : base + NZ, :] = value
        field[base - 1 : base, :] = value[NZ - 1 : NZ, :]
        field[base + NZ : base + NZ + 1, :] = value[0:1, :]

    for number in range(0, 20, 2):
        columns = [column(in_ref, number + step, count) for step in range(2)]
        both = left_mul(z_ref, jnp.concatenate(columns, axis=1))
        put(number, both[:, :128])
        put(number + 1, both[:, 128:])
    put(20, left_mul(z_ref, column(in_ref, 20, count)))


def slopes(field, part, x, z, lane):
    def rows(number, step=0):
        return field[pl.ds(number * COLUMN + 8 + z + step, CHUNK), :]

    number = part * 10 + x + 1
    here, edge = rows(number), rows(20)
    spot = 2 * (part * 8 + x)
    below = jnp.where(lane == 0, pltpu.roll(edge, (128 - spot) % 128, 1), pltpu.roll(here, 1, 1))
    above = jnp.where(lane == 127, pltpu.roll(edge, 126 - spot, 1), pltpu.roll(here, 127, 1))
    others = [rows(number - 1), rows(number + 1), above, below, rows(number, 1), rows(number, -1)]
    return here, [here - other for other in others]


def weights(faces_ref, ends_ref, x, z, kappa):
    rows = pl.ds(z, CHUNK)
    low = ends_ref[0, rows, :] if x == 0 else faces_ref[x, rows, :]
    high = ends_ref[1, rows, :] if x == 7 else faces_ref[x + 1, rows, :]
    terms = [low, high] + [faces_ref[8 * number + 1 + x, rows, :] for number in range(1, 5)]
    return [term - kappa for term in terms]


def weighted(terms, values):
    total = [term * value for term, value in zip(terms, values)]
    return ((total[0] + total[1]) + (total[2] + total[3])) + (total[4] + total[5])


def block_first_kernel(place_ref, kappa_ref, in_ref, z_ref, faces_ref, out_ref, differ_ref, image_ref, ends_ref, field):
    kappa = kappa_ref[0:1, 0:1]
    pair = place_ref[0] // 2
    real = [jnp.float32(shift_of(4 * part)[0]) for part in range(2)]
    imag = jnp.float32(0.0)
    for number in range(1, 4):
        real = [jnp.where(pair == number, shift_of(number)[0], value) for value in real]
        imag = jnp.where(pair == number, shift_of(number)[1], imag)
    load_block(in_ref, z_ref, field, ROWS_FIRST)
    ends_ref[0] = 0.5 * (column(in_ref, 21, ROWS_FIRST) + faces_ref[0])
    ends_ref[1] = 0.5 * (column(in_ref, 22, ROWS_FIRST) + faces_ref[8])
    lane = lax.broadcasted_iota(jnp.int32, (CHUNK, 128), 1)
    for x in range(8):
        for z in range(0, NZ, CHUNK):
            terms = weights(faces_ref, ends_ref, x, z, kappa)
            cells = [slopes(field, part, x, z, lane) for part in range(2)]
            for part in range(2):
                here, slope = cells[part]
                value = weighted(terms, slope)
                differ_ref[part, x, pl.ds(z, CHUNK), :] = value
                cross = -imag if part == 0 else imag
                image_ref[part, x, pl.ds(z, CHUNK), :] = value + (
                    real[part] * here
                    + cross * cells[1 - part][0]
                    + (step_length * kappa)
                    * (((slope[0] + slope[1]) + (slope[2] + slope[3])) + (slope[4] + slope[5]))
                )
        freq = left_mul(z_ref, jnp.concatenate([differ_ref[0, x], differ_ref[1, x]], axis=1))
        for part in range(2):
            for block in range(16):
                out_ref[pl.ds(block * 8 * 16 + part * 8 + x, 8, stride=16), :] = freq[
                    block * 8 : block * 8 + 8, part * 128 : part * 128 + 128
                ]


def block_second_kernel(
    kappa_ref, in_ref, differ_ref, image_ref, z_ref, faces_ref, ends_ref, out_ref, field
):
    kappa = kappa_ref[0:1, 0:1]
    load_block(in_ref, z_ref, field, ROWS)
    lane = lax.broadcasted_iota(jnp.int32, (CHUNK, 128), 1)
    totals = [jnp.zeros((8, 128), f32) for _ in range(16)]

    def fold(value):
        return jnp.sum(value.reshape(CHUNK // 8, 8, 128), axis=0)

    for x in range(8):
        for z in range(0, NZ, CHUNK):
            terms = weights(faces_ref, ends_ref, x, z, kappa)
            diffs = [differ_ref[part, x, pl.ds(z, CHUNK), :] for part in range(2)]
            ones = [image_ref[part, x, pl.ds(z, CHUNK), :] for part in range(2)]
            twos = [diffs[part] + weighted(terms, slopes(field, part, x, z, lane)[1]) for part in range(2)]
            pairs = [(ones[0], ones[0]), (ones[1], ones[1]), (twos[0], twos[0]), (twos[1], twos[1])]
            for left, right in ((ones, twos), (ones, diffs), (twos, diffs)):
                pairs += [(left[0], right[0]), (left[1], right[1]), (left[0], right[1]), (left[1], right[0])]
            for number, (left, right) in enumerate(pairs):
                totals[number] = totals[number] + fold(left * right)
    spot = lax.broadcasted_iota(jnp.int32, (1, 128), 1)
    row = jnp.zeros((1, 128), f32)
    for number in range(16):
        row = row + jnp.where(spot == number, jnp.sum(totals[number], keepdims=True), 0.0)
    out_ref[...] = jnp.broadcast_to(row, (DEVS, 128))


def leave_kernel(in_ref, z_ref, out_hbm, out_ref, sems):
    copies = [pltpu.make_async_copy(out_ref.at[x], out_hbm.at[0, x], sems.at[x]) for x in range(8)]
    for x in range(8):
        columns = []
        for yh in range(2):
            rows = [in_ref[pl.ds(block * 8 * 16 + yh * 8 + x, 8, stride=16), :] for block in range(16)]
            columns.append(jnp.concatenate(rows, axis=0))
        value = left_mul(z_ref, jnp.concatenate(columns, axis=1))
        out_ref[x] = value.T
        copies[x].start()
    for copy in copies:
        copy.wait()


def exchange(rows):
    wide = rows.reshape(rows.shape[0], 1, 128)
    return lax.all_to_all(wide, BOTH, split_axis=0, concat_axis=0, tiled=True).reshape(rows.shape)


def call(kernel, outs, scalars, scratch, *args, far_in=(), far_out=()):
    args = [
        pltpu.with_memory_space_constraint(arg, pltpu.HBM) if number in far_in else arg
        for number, arg in enumerate(args)
    ]
    outs = [pltpu.HBM(out.shape, out.dtype) if number in far_out else out for number, out in enumerate(outs)]
    return pl.pallas_call(
        kernel,
        out_shape=outs,
        in_specs=[
            smem() if number < scalars else (hbm() if number in far_in else vmem()) for number in range(len(args))
        ],
        out_specs=[hbm() if number in far_out else vmem() for number in range(len(outs))],
        scratch_shapes=scratch,
        name=kernel.__name__,
        compiler_params=pltpu.CompilerParams(vmem_limit_bytes=16 << 20),
    )(*args)


def shards(source, initial, diffusivity):
    table = tables()
    position = lax.axis_index("tm")
    slab = lax.axis_index("space")
    wave = (position * SLABS + slab).astype(f32)
    symbol_z = (4.0 * jnp.sin(math.pi * wave / NZ) ** 2).reshape(1)
    place = position.astype(jnp.int32).reshape(1)
    source, place, symbol_z = lax.optimization_barrier((source, place, symbol_z))

    slab_block = pltpu.VMEM((8, NY, NZ), f32)
    (rows,) = call(
        enter_kernel,
        [shape(DEVS * 17, 128)],
        1,
        [
            slab_block,
            slab_block,
            pltpu.VMEM((2, NY, NZ), f32),
            pltpu.VMEM((128, NZ), f32),
            pltpu.VMEM((2, NZ, NZ), bf16),
            pltpu.SemaphoreType.DMA((19,)),
        ],
        place,
        source[0],
        initial,
        diffusivity,
        table["z"],
        far_in=(1, 2, 3, 4),
    )
    rows = exchange(rows)
    big = pltpu.VMEM((1024, NY), f32)
    hat_one, rows, kappa = call(
        spectral_first_kernel,
        [shape(1024, NY), shape(DEVS * ROWS_FIRST, 128), shape(8, 128)],
        1,
        [big, big],
        symbol_z,
        rows,
        table["spectral"],
        table["symbol"],
    )
    rows, diffusivity = lax.optimization_barrier((rows, diffusivity))
    (faces,) = call(faces_kernel, [shape(41, NZ, 128)], 1, [], place, diffusivity)
    rows, faces = lax.optimization_barrier((rows, faces))
    rows = exchange(rows)
    block = pltpu.VMEM((21 * COLUMN, 128), f32)
    rows, differ, right, ends = call(
        block_first_kernel,
        [shape(DEVS * 16, 128), shape(2, 8, NZ, 128), shape(2, 8, NZ, 128), shape(2, NZ, 128)],
        1,
        [block],
        place,
        kappa,
        rows,
        table["z"],
        faces,
    )
    rows = exchange(rows)
    hat_two, rows = call(
        spectral_second_kernel,
        [shape(1024, NY), shape(DEVS * ROWS, 128)],
        1,
        [big, big],
        symbol_z,
        kappa,
        rows,
        table["spectral"],
        table["symbol"],
    )
    rows = exchange(rows)
    (sums,) = call(block_second_kernel, [shape(DEVS, 128)], 0, [block], kappa, rows, differ, right, table["z"], faces, ends)
    sums, hat_one, hat_two = lax.optimization_barrier((sums, hat_one, hat_two))
    sums = exchange(sums)
    one, two = call(
        unfold_kernel, [shape(1024, NY), shape(1024, NY)], 0, [big], hat_one, hat_two, table["x"], table["y"]
    )
    (rows,) = call(combine_kernel, [shape(DEVS * 16, 128)], 0, [], sums, one, two)
    rows = exchange(rows)
    (field,) = call(
        leave_kernel,
        [shape(1, 8, NY, NZ)],
        0,
        [slab_block, pltpu.SemaphoreType.DMA((8,))],
        rows,
        table["z"],
        far_out=(0,),
    )
    return field


def solution(mesh):
    in_specs = (P("tm", "space", None, None), P("space", None, None), P("space", None, None))
    out_specs = P("tm", "space", None, None)
    return jax.shard_map(shards, mesh=mesh, in_specs=in_specs, out_specs=out_specs, check_vma=False)
```
